128 devices in a mesh: frame: 32 (over z, x, y_lo), row: 2 (over y_hi), col: 2 (over core).
Axes of the slice: x: 4, y: 4 (y_hi: 2, y_lo: 2; y = y_hi * 2 + y_lo), z: 4, core: 2. Of those that a mesh axis runs over, the one named last changes fastest.
Arguments:
- measurement: float32 [1024, 2048], P('row', 'col'), may hold values from 0 to 4
- masks: float32 [32, 1024, 2048], P('frame', 'row', 'col'), may hold values from 0.1 to 1
- estimate: float32 [32, 1024, 2048], P('frame', 'row', 'col'), may hold values from 0 to 1
Outputs:
- video: float32 [32, 1024, 2048], P('frame', 'row', 'col')
The draws below stay inside these ranges and needn't reach their ends.
All inputs are finite; a program needn't handle non-finite values.
Results may differ from the reference program's by a relative error of at most 0.0001.
Values sent between devices are 32-bit elements; how exact they have to be, the bound alone decides.
No kernel may reach another device: no remote copies, remote signals or barrier semaphores. Data moves between devices by JAX's collectives and lax.ppermute only.
A program may use at most 64 MiB of HBM per device.

```python
import jax
import jax.numpy as jnp
from jax import lax

PROJ = 2
TV_ITERS = 5
FRAMES = 32
HEIGHT = 1024
WIDTH = 2048


def steps_of(key, dims, shards, smallest, largest):
    loudness, own = 1.0, jax.random.fold_in(key, 6)
    for dim, shards_of in shards:
        steps = jnp.exp(jax.random.uniform(jax.random.fold_in(own, dim), (shards_of,), jnp.float32, smallest / len(shards), largest / len(shards)))
        loudness = loudness * jnp.repeat(steps, dims[dim] // shards_of).reshape([-1 if axis == dim else 1 for axis in range(len(dims))])
    return loudness


def setup_inputs(seed: int = 0) -> dict:
    arg_keys = jax.random.split(jax.random.key(seed), 4)
    return {
        "measurement": jnp.clip(4.0 * jax.random.uniform(arg_keys[0], (HEIGHT, WIDTH), jnp.float32) ** steps_of(arg_keys[0], (HEIGHT, WIDTH), ((0, 2), (1, 2)), -0.2, 0.2), 0.0, 4.0),
        "masks": jnp.clip(0.1 + 0.9 * jax.random.uniform(arg_keys[1], (FRAMES, HEIGHT, WIDTH), jnp.float32) ** steps_of(arg_keys[1], (FRAMES, HEIGHT, WIDTH), ((0, 32), (1, 2), (2, 2)), -0.2, 0.2), 0.1, 1.0),
        "estimate": jnp.clip(1.0 * jax.random.uniform(arg_keys[2], (FRAMES, HEIGHT, WIDTH), jnp.float32) ** steps_of(arg_keys[2], (FRAMES, HEIGHT, WIDTH), ((0, 32), (1, 2), (2, 2)), -0.2, 0.2), 0.0, 1.0),
    }


tv_weight = 0.1
step_size = 0.125

def gradient(field):
    frames = field.shape[0]
    zero_row = jnp.zeros((frames, 1, field.shape[2]), jnp.float32)
    zero_col = jnp.zeros((frames, field.shape[1], 1), jnp.float32)
    grad_rows = jnp.concatenate([field[:, 1:, :] - field[:, :-1, :], zero_row], 1)
    grad_cols = jnp.concatenate([field[:, :, 1:] - field[:, :, :-1], zero_col], 2)
    return (grad_rows, grad_cols)

def divergence(flux_rows, flux_cols):
    frames = flux_rows.shape[0]
    zero_row = jnp.zeros((frames, 1, flux_rows.shape[2]), jnp.float32)
    zero_col = jnp.zeros((frames, flux_cols.shape[1], 1), jnp.float32)
    above = jnp.concatenate([zero_row, flux_rows[:, :-1, :]], 1)
    left = jnp.concatenate([zero_col, flux_cols[:, :, :-1]], 2)
    return flux_rows - above + flux_cols - left

def denoise(noisy):
    flux_rows = jnp.zeros_like(noisy)
    flux_cols = jnp.zeros_like(noisy)
    for step in range(TV_ITERS):
        dual = divergence(flux_rows, flux_cols) - noisy / tv_weight
        grad_rows, grad_cols = gradient(dual)
        magnitude = jnp.sqrt(grad_rows * grad_rows + grad_cols * grad_cols)
        scaling = 1.0 + step_size * magnitude
        flux_rows = (flux_rows + step_size * grad_rows) / scaling
        flux_cols = (flux_cols + step_size * grad_cols) / scaling
    return noisy - tv_weight * divergence(flux_rows, flux_cols)

def reference(measurement, masks, estimate):
    weights = masks
    count = lax.optimization_barrier(jnp.sum(weights * weights, 0))
    video = estimate
    for step in range(PROJ):
        measured = lax.optimization_barrier(jnp.sum(weights * video, 0))
        video = video + weights * ((measurement - measured) / count)[None]
        video = denoise(video)
    return video
```

```python
import jax
import jax.numpy as jnp
from jax import lax
from jax.experimental import pallas as pl
from jax.experimental.pallas import tpu as pltpu
from jax.sharding import PartitionSpec as P

PROJ = 2
TV_ITERS = 5

tv_weight = 0.1
step_size = 0.125

ROWS = 512
COLS = 1024
HR = 8
HC = 128
SUB = 8


def shifted(level, distance):
    pairs = []
    for frame in range(32):
        z, x, y = frame // 8, (frame // 2) % 4, frame % 2
        for core in range(2):
            tz, tx, ty = z, x, y
            if level == 2:
                ty = (y + distance) % 2
            elif (level == 0) == (core == 0):
                tz = (z + distance) % 4
            else:
                tx = (x + distance) % 4
            pairs.append((frame * 2 + core, (tz * 8 + tx * 2 + ty) * 2 + core))
    return pairs


def hop(block, level, distance):
    return lax.ppermute(block, ("frame", "col"), shifted(level, distance))


def positions():
    frame = lax.axis_index("frame")
    core = lax.axis_index("col")
    z, x, y = frame // 8, (frame // 2) % 4, frame % 2
    return (jnp.where(core == 0, z, x), jnp.where(core == 0, x, z), y)


def piece(field, index, size):
    return lax.dynamic_slice_in_dim(field, index * size, size, field.ndim - 2)


def reduce_scatter(field):
    for level, (place, parts) in enumerate(zip(positions(), (4, 4, 2))):
        size = field.shape[-2] // parts
        got = [piece(field, place, size)]
        for distance in (1, 3, 2)[: parts - 1]:
            got.append(hop(piece(field, (place + distance) % parts, size), level, distance))
        field = sum(got[1:], got[0])
    return field


def gather(field):
    for level, place, parts in reversed(list(zip(range(3), positions(), (4, 4, 2)))):
        size = field.shape[-2]
        whole = jnp.zeros(field.shape[:-2] + (size * parts, field.shape[-1]), field.dtype)
        got = {0: field}
        for distance in (1, 3, 2)[: parts - 1]:
            got[distance] = hop(field, level, distance)
        for distance, block in got.items():
            source = (place - distance) % parts
            whole = lax.dynamic_update_slice_in_dim(whole, block, source * size, field.ndim - 2)
        field = whole
    return field


def tv_kernel(edge_ref, video_ref, masks_ref, ratio_ref, below_ref, beside_ref, corner_ref, out_ref, prod_ref, f_ref, pr_ref, pc_ref):
    rows, cols = f_ref.shape
    blocks = rows // SUB
    row_edge = edge_ref[0]
    col_edge = edge_ref[1]
    scale = step_size / tv_weight
    f_ref[:ROWS, :COLS] = scale * (video_ref[...] + masks_ref[...] * ratio_ref[...])
    f_ref[ROWS:, :COLS] = scale * below_ref[...]
    f_ref[:ROWS, COLS:] = scale * beside_ref[...]
    f_ref[ROWS:, COLS:] = scale * corner_ref[...]
    sub = lax.broadcasted_iota(jnp.int32, (SUB, cols), 0)
    lane = lax.broadcasted_iota(jnp.int32, (SUB, cols), 1)
    col_keep = jnp.where(lane == col_edge, 0.0, 1.0)

    def at(ref, k):
        return ref[pl.ds(pl.multiple_of(k * SUB, SUB), SUB), :]

    def put(ref, k, value):
        ref[pl.ds(pl.multiple_of(k * SUB, SUB), SUB), :] = value

    def dual(k, pr, pr_before, pc):
        up = pltpu.roll(jnp.where(sub == SUB - 1, pr_before, pr), 1, 0)
        left = pltpu.roll(pc, 1, 1)
        return step_size * (pr - up + pc - left) - at(f_ref, k)

    def update(k, w, w_next, pr, pc):
        down = pltpu.roll(jnp.where(sub == 0, w_next, w), SUB - 1, 0)
        right = pltpu.roll(w, cols - 1, 1)
        gr = jnp.where(sub == row_edge - k * SUB, 0.0, down - w)
        gc = (right - w) * col_keep
        s = gr * gr + gc * gc
        inv = 1.0 / (1.0 + jnp.sqrt(s))
        if pr is None:
            return gr * inv, gc * inv
        return (pr + gr) * inv, (pc + gc) * inv

    def first(k, w):
        w_next = -at(f_ref, lax.rem(k + 1, blocks))
        pr, pc = update(k, w, w_next, None, None)
        put(pr_ref, k, pr)
        put(pc_ref, k, pc)
        return w_next

    lax.fori_loop(0, blocks, first, -at(f_ref, 0))

    def iteration(_, carry):
        pr0 = at(pr_ref, 0)
        w0 = dual(0, pr0, at(pr_ref, blocks - 1), at(pc_ref, 0))

        def body(k, carry):
            w, pr, pc = carry
            pr_next = at(pr_ref, k + 1)
            pc_next = at(pc_ref, k + 1)
            w_next = dual(k + 1, pr_next, pr, pc_next)
            pr_new, pc_new = update(k, w, w_next, pr, pc)
            put(pr_ref, k, pr_new)
            put(pc_ref, k, pc_new)
            return w_next, pr_next, pc_next

        w, pr, pc = lax.fori_loop(0, blocks - 1, body, (w0, pr0, at(pc_ref, 0)))
        pr_new, pc_new = update(blocks - 1, w, w0, pr, pc)
        put(pr_ref, blocks - 1, pr_new)
        put(pc_ref, blocks - 1, pc_new)
        return carry

    lax.fori_loop(1, TV_ITERS, iteration, 0)

    def last(k, pr_before):
        pr = at(pr_ref, k)
        w = dual(k, pr, pr_before, at(pc_ref, k))
        video = (-tv_weight / step_size) * w[:, :COLS]
        put(out_ref, k, video)
        put(prod_ref, k, video * at(masks_ref, k))
        return pr

    lax.fori_loop(0, ROWS // SUB, last, at(pr_ref, blocks - 1))


def denoise(video, masks, ratio):
    row = lax.axis_index("row")
    col = lax.axis_index("col")

    def noisy(r0, rn, c0, cn):
        cut = lambda a: lax.dynamic_slice(a, (r0, c0), (rn, cn))
        return cut(video) + cut(masks) * cut(ratio)

    r0 = jnp.where(row == 0, ROWS - HR, 0)
    c0 = jnp.where(col == 0, COLS - HC, 0)
    swap = [(0, 1), (1, 0)]
    below = lax.ppermute(noisy(r0, HR, 0, COLS), "row", swap)
    corner = lax.ppermute(noisy(r0, HR, c0, HC), ("row", "col"), [(0, 3), (3, 0), (1, 2), (2, 1)])
    beside = lax.ppermute(noisy(0, ROWS, c0, HC), "col", swap)
    rows, cols = ROWS + HR, COLS + HC
    edges = jnp.stack([jnp.where(row == 0, rows, ROWS) - 1, jnp.where(col == 0, cols, COLS) - 1]).astype(jnp.int32)
    whole = jax.ShapeDtypeStruct((ROWS, COLS), jnp.float32)
    vmem = pl.BlockSpec(memory_space=pltpu.VMEM)
    return pl.pallas_call(
        tv_kernel,
        out_shape=(whole, whole),
        in_specs=[pl.BlockSpec(memory_space=pltpu.SMEM)] + [vmem] * 6,
        out_specs=(vmem, vmem),
        scratch_shapes=[pltpu.VMEM((rows, cols), jnp.float32)] * 3,
        name="tv",
    )(edges, video, masks, ratio, below, beside, corner)


def per_device(measurement, masks, estimate):
    masks = masks[0]
    video = estimate[0]
    place1, place2, place3 = positions()
    sensor = piece(piece(piece(measurement, place1, 128), place2, 32), place3, 16)
    sums = reduce_scatter(jnp.stack([masks * masks, masks * video]))
    count = sums[0]
    measured = sums[1]
    for step in range(PROJ):
        ratio = gather((sensor - measured) / count)
        video, product = denoise(video, masks, ratio)
        if step < PROJ - 1:
            measured = reduce_scatter(product)
    return video[None]


def solution(mesh):
    return jax.shard_map(
        per_device,
        mesh=mesh,
        in_specs=(P("row", "col"), P("frame", "row", "col"), P("frame", "row", "col")),
        out_specs=P("frame", "row", "col"),
        check_vma=False,
    )
```

```python
import jax
import jax.numpy as jnp
from jax import lax
from jax.experimental import pallas as pl
from jax.experimental.pallas import tpu as pltpu
from jax.sharding import PartitionSpec as P

PROJ = 2
TV_ITERS = 5

tv_weight = 0.1
step_size = 0.125

ROWS = 512
COLS = 1024
HR = 8
HC = 128
SUB = 104
TINY = 1e-35


def shifted(level, distance):
    pairs = []
    for frame in range(32):
        z, x, y = frame // 8, (frame // 2) % 4, frame % 2
        for core in range(2):
            tz, tx, ty = z, x, y
            if level == 2:
                ty = (y + distance) % 2
            elif (level == 0) == (core == 0):
                tz = (z + distance) % 4
            else:
                tx = (x + distance) % 4
            pairs.append((frame * 2 + core, (tz * 8 + tx * 2 + ty) * 2 + core))
    return pairs


def hop(block, level, distance):
    return lax.ppermute(block, ("frame", "col"), shifted(level, distance))


def positions():
    frame = lax.axis_index("frame")
    core = lax.axis_index("col")
    z, x, y = frame // 8, (frame // 2) % 4, frame % 2
    return (jnp.where(core == 0, z, x), jnp.where(core == 0, x, z), y)


def piece(field, index, size):
    return lax.dynamic_slice_in_dim(field, index * size, size, field.ndim - 2)


def reduce_scatter(field):
    for level, (place, parts) in enumerate(zip(positions(), (4, 4, 2))):
        size = field.shape[-2] // parts
        got = [piece(field, place, size)]
        for distance in (1, 3, 2)[: parts - 1]:
            got.append(hop(piece(field, (place + distance) % parts, size), level, distance))
        field = sum(got[1:], got[0])
    return field


def gather(field):
    for level, place, parts in reversed(list(zip(range(3), positions(), (4, 4, 2)))):
        size = field.shape[-2]
        whole = jnp.zeros(field.shape[:-2] + (size * parts, field.shape[-1]), field.dtype)
        got = {0: field}
        for distance in (1, 3, 2)[: parts - 1]:
            got[distance] = hop(field, level, distance)
        for distance, block in got.items():
            source = (place - distance) % parts
            whole = lax.dynamic_update_slice_in_dim(whole, block, source * size, field.ndim - 2)
        field = whole
    return field


def tv_kernel(edge_ref, video_ref, masks_ref, ratio_ref, below_ref, beside_ref, corner_ref, out_ref, prod_ref, f_ref, pr_ref, pc_ref, w_ref):
    tiles, rows, lanes = f_ref.shape
    row_at = edge_ref[0]
    tile_at = edge_ref[1]
    scale = step_size / tv_weight
    halo_row = pl.multiple_of(jnp.where(row_at == 0, ROWS, 0), HR)
    halo_tile = jnp.where(tile_at == 0, tiles - 1, 0)
    core_row = pl.multiple_of(row_at, HR)
    lane = lax.broadcasted_iota(jnp.int32, (SUB, lanes), 1)

    def load_core(k, carry):
        r = pl.multiple_of(k * 64, 64)
        to = pl.multiple_of(row_at + r, HR)
        for t in range(tiles - 1):
            cut = (pl.ds(r, 64), slice(t * lanes, (t + 1) * lanes))
            f_ref[tile_at + t, pl.ds(to, 64), :] = scale * (video_ref[cut] + masks_ref[cut] * ratio_ref[cut])
        f_ref[halo_tile, pl.ds(to, 64), :] = scale * beside_ref[pl.ds(r, 64), :]
        return carry

    lax.fori_loop(0, ROWS // 64, load_core, 0)
    for t in range(tiles - 1):
        f_ref[tile_at + t, pl.ds(halo_row, HR), :] = scale * below_ref[:, t * lanes : (t + 1) * lanes]
    f_ref[halo_tile, pl.ds(halo_row, HR), :] = scale * corner_ref[...]
    pr_ref[:, :HR, :] = jnp.zeros((tiles, HR, lanes), jnp.float32)

    def make_dual(k, carry):
        r = pl.multiple_of(k * SUB, SUB)
        before = 0.0
        for t in range(tiles):
            pc = pc_ref[t, pl.ds(r, SUB), :]
            turned = pltpu.roll(pc, 1, 1)
            left = jnp.where(lane == 0, before, turned)
            before = turned
            pr = pr_ref[t, pl.ds(r + HR, SUB), :]
            up = pr_ref[t, pl.ds(r + HR - 1, SUB), :]
            w_ref[t, pl.ds(r, SUB), :] = step_size * ((pr - up) + (pc - left)) - f_ref[t, pl.ds(r, SUB), :]
        return carry

    def pin_last_row():
        w_ref[:, rows : rows + 1, :] = w_ref[:, rows - 1 : rows, :]

    def make_update(start):
        def body(k, carry):
            r = pl.multiple_of(k * SUB, SUB)
            w = [w_ref[t, pl.ds(r, SUB), :] for t in range(tiles)]
            turned = [pltpu.roll(w[t], lanes - 1, 1) for t in range(tiles)]
            for t in range(tiles):
                right = jnp.where(lane == lanes - 1, turned[t + 1] if t + 1 < tiles else w[t], turned[t])
                gr = w_ref[t, pl.ds(r + 1, SUB), :] - w[t]
                gc = right - w[t]
                s = gr * gr + gc * gc
                inv = 1.0 / (1.0 + s * lax.rsqrt(jnp.maximum(s, TINY)))
                if not start:
                    gr = pr_ref[t, pl.ds(r + HR, SUB), :] + gr
                    gc = pc_ref[t, pl.ds(r, SUB), :] + gc
                pr_ref[t, pl.ds(r + HR, SUB), :] = gr * inv
                pc_ref[t, pl.ds(r, SUB), :] = gc * inv
            return carry

        return body

    def first(k, carry):
        r = pl.multiple_of(k * SUB, SUB)
        for t in range(tiles):
            w_ref[t, pl.ds(r, SUB), :] = -f_ref[t, pl.ds(r, SUB), :]
        return carry

    lax.fori_loop(0, rows // SUB, first, 0)
    pin_last_row()
    lax.fori_loop(0, rows // SUB, make_update(True), 0)

    def iteration(_, carry):
        lax.fori_loop(0, rows // SUB, make_dual, 0)
        pin_last_row()
        lax.fori_loop(0, rows // SUB, make_update(False), 0)
        return carry

    lax.fori_loop(1, TV_ITERS, iteration, 0)
    lax.fori_loop(0, rows // SUB, make_dual, 0)

    def last(k, carry):
        r = pl.multiple_of(k * 64, 64)
        of = pl.multiple_of(row_at + r, HR)
        for t in range(tiles - 1):
            cut = (pl.ds(r, 64), slice(t * lanes, (t + 1) * lanes))
            video = (-tv_weight / step_size) * w_ref[tile_at + t, pl.ds(of, 64), :]
            out_ref[cut] = video
            prod_ref[cut] = video * masks_ref[cut]
        return carry

    lax.fori_loop(0, ROWS // 64, last, 0)


def denoise(video, masks, ratio):
    row = lax.axis_index("row")
    col = lax.axis_index("col")

    def noisy(r0, rn, c0, cn):
        cut = lambda a: lax.dynamic_slice(a, (r0, c0), (rn, cn))
        return cut(video) + cut(masks) * cut(ratio)

    r0 = jnp.where(row == 0, ROWS - HR, 0)
    c0 = jnp.where(col == 0, COLS - HC, 0)
    swap = [(0, 1), (1, 0)]
    below = lax.ppermute(noisy(r0, HR, 0, COLS), "row", swap)
    corner = lax.ppermute(noisy(r0, HR, c0, HC), ("row", "col"), [(0, 3), (3, 0), (1, 2), (2, 1)])
    beside = lax.ppermute(noisy(0, ROWS, c0, HC), "col", swap)
    edges = jnp.stack([row * HR, col]).astype(jnp.int32)
    rows, tiles = ROWS + HR, (COLS + HC) // HC
    held = pltpu.VMEM((tiles, rows, HC), jnp.float32)
    padded = pltpu.VMEM((tiles, rows + HR, HC), jnp.float32)
    whole = jax.ShapeDtypeStruct((ROWS, COLS), jnp.float32)
    vmem = pl.BlockSpec(memory_space=pltpu.VMEM)
    return pl.pallas_call(
        tv_kernel,
        out_shape=(whole, whole),
        in_specs=[pl.BlockSpec(memory_space=pltpu.SMEM)] + [vmem] * 6,
        out_specs=(vmem, vmem),
        scratch_shapes=[held, padded, held, padded],
        name="tv",
    )(edges, video, masks, ratio, below, beside, corner)


def per_device(measurement, masks, estimate):
    masks = masks[0]
    video = estimate[0]
    place1, place2, place3 = positions()
    sensor = piece(piece(piece(measurement, place1, 128), place2, 32), place3, 16)
    sums = reduce_scatter(jnp.stack([masks * masks, masks * video]))
    count = sums[0]
    measured = sums[1]
    for step in range(PROJ):
        ratio = gather((sensor - measured) / count)
        video, product = denoise(video, masks, ratio)
        if step < PROJ - 1:
            measured = reduce_scatter(product)
    return video[None]


def solution(mesh):
    return jax.shard_map(
        per_device,
        mesh=mesh,
        in_specs=(P("row", "col"), P("frame", "row", "col"), P("frame", "row", "col")),
        out_specs=P("frame", "row", "col"),
        check_vma=False,
    )
```

```python
import jax
import jax.numpy as jnp
from jax import lax
from jax.experimental import pallas as pl
from jax.experimental.pallas import tpu as pltpu
from jax.sharding import PartitionSpec as P

PROJ = 2
TV_ITERS = 5

tv_weight = 0.1
step_size = 0.125

ROWS = 512
COLS = 1024
QUARTER = ROWS // 4
HR = 16
HC = 128
WINDOW = QUARTER + 2 * HR
WIDE = COLS + HC
TILES = WIDE // HC
CHUNK = WINDOW // 4
PAD = 8
TINY = 1e-35
TURNS = (1, 3, 2)


VMEM = pl.BlockSpec(memory_space=pltpu.VMEM)
SMEM = pl.BlockSpec(memory_space=pltpu.SMEM)


def f32(*shape):
    return jax.ShapeDtypeStruct(shape, jnp.float32)


def shifted(level, distance):
    pairs = []
    for frame in range(32):
        z, x, y = frame // 8, (frame // 2) % 4, frame % 2
        for core in range(2):
            tz, tx, ty = z, x, y
            if level == 2:
                ty = (y + distance) % 2
            elif (level == 0) == (core == 0):
                tz = (z + distance) % 4
            else:
                tx = (x + distance) % 4
            pairs.append((frame * 2 + core, (tz * 8 + tx * 2 + ty) * 2 + core))
    return pairs


def hop(block, level, distance):
    return lax.ppermute(block, ("frame", "col"), shifted(level, distance))


def window_start(quarter, row):
    return jnp.clip(quarter * QUARTER + row * HR - HR, 0, ROWS + HR - WINDOW)


def pack_kernel(at_ref, masks_ref, video_ref, sensor_ref, beside_ref, below_ref, *refs):
    outs, sensor_out, all_ref = refs[:4], refs[4], refs[5]
    row = at_ref[0]
    col = at_ref[1]
    own_row = pl.multiple_of(row * HR, HR)
    other_row = pl.multiple_of((1 - row) * ROWS, HR)
    own_col = pl.multiple_of(col * HC, HC)
    other_col = pl.multiple_of((1 - col) * COLS, HC)
    for n, source in enumerate((masks_ref, video_ref, sensor_ref)):
        all_ref[pl.ds(own_row, ROWS), pl.ds(own_col, COLS)] = source[...]
        all_ref[pl.ds(own_row, ROWS), pl.ds(other_col, HC)] = beside_ref[n]
        all_ref[pl.ds(other_row, HR), :] = below_ref[n]
        if n < 2:
            for k in range(4):
                outs[k][n] = all_ref[pl.ds(pl.multiple_of(at_ref[2 + k], HR), WINDOW), :]
        else:
            sensor_out[...] = all_ref[pl.ds(pl.multiple_of(at_ref[2], HR), WINDOW), :]


def pack(at, masks, video, sensor, beside, below):
    window = f32(2, WINDOW, WIDE)
    return pl.pallas_call(
        pack_kernel,
        out_shape=(window,) * 4 + (f32(WINDOW, WIDE),),
        in_specs=[SMEM] + [VMEM] * 5,
        out_specs=(VMEM,) * 5,
        scratch_shapes=[pltpu.VMEM((ROWS + HR, WIDE), jnp.float32)],
        name="pack",
    )(at, masks, video, sensor, beside, below)


def tally_kernel(*refs):
    frames, out_ref = refs[:4], refs[4]
    count = 0.0
    measured = 0.0
    for frame in frames:
        masks = frame[0]
        count += masks * masks
        measured += masks * frame[1]
    out_ref[0] = count
    out_ref[1] = measured


def tally(frames):
    return pl.pallas_call(
        tally_kernel,
        out_shape=f32(2, WINDOW, WIDE),
        in_specs=[VMEM] * 4,
        out_specs=VMEM,
        name="tally",
    )(*frames)


def tv_steps(f_ref, pr_ref, pc_ref, w_ref, frame):
    tiles, rows, lanes = f_ref.shape[1:]
    lane = lax.broadcasted_iota(jnp.int32, (rows, lanes), 1)

    def dual():
        before = 0.0
        for t in range(tiles):
            pc = pc_ref[t]
            turned = pltpu.roll(pc, 1, 1)
            left = jnp.where(lane == 0, before, turned)
            before = turned
            pr = pr_ref[t, PAD : PAD + rows, :]
            up = pr_ref[t, PAD - 1 : PAD - 1 + rows, :]
            w_ref[t, :rows, :] = step_size * ((pr - up) + (pc - left)) - f_ref[frame, t]
        w_ref[:, rows : rows + 1, :] = w_ref[:, rows - 1 : rows, :]

    def update(start):
        turned = pltpu.roll(w_ref[0, :rows, :], lanes - 1, 1)
        for t in range(tiles):
            w = w_ref[t, :rows, :]
            following = pltpu.roll(w_ref[t + 1, :rows, :], lanes - 1, 1) if t + 1 < tiles else w
            right = jnp.where(lane == lanes - 1, following, turned)
            turned = following
            gr = w_ref[t, 1 : rows + 1, :] - w
            gc = right - w
            s = gr * gr + gc * gc
            inv = 1.0 / (1.0 + s * lax.rsqrt(jnp.maximum(s, TINY)))
            if not start:
                gr = pr_ref[t, PAD : PAD + rows, :] + gr
                gc = pc_ref[t] + gc
            pr_ref[t, PAD : PAD + rows, :] = gr * inv
            pc_ref[t] = gc * inv

    for t in range(tiles):
        w_ref[t, :rows, :] = -f_ref[frame, t]
    w_ref[:, rows : rows + 1, :] = w_ref[:, rows - 1 : rows, :]
    update(True)

    def iteration(_, carry):
        dual()
        update(False)
        return carry

    lax.fori_loop(1, TV_ITERS, iteration, 0)
    dual()


def load_ratio(at_ref, ratios, ratio_ref):
    for k, ratio in enumerate(ratios):
        ratio_ref[pl.ds(pl.multiple_of(at_ref[k], PAD), CHUNK), :] = ratio[...]


def first_kernel(at_ref, *refs):
    frames, ratios, videos, product_ref = refs[:4], refs[4:8], refs[8:12], refs[12]
    ratio_ref, f_ref, pr_ref, pc_ref, w_ref = refs[13:]
    load_ratio(at_ref, ratios, ratio_ref)
    scale = step_size / tv_weight
    pr_ref[:, :PAD, :] = jnp.zeros((TILES, PAD, HC), jnp.float32)
    for k, frame in enumerate(frames):
        for t in range(TILES):
            cut = (slice(None), slice(t * HC, (t + 1) * HC))
            f_ref[k, t] = scale * (frame[(1,) + cut] + frame[(0,) + cut] * ratio_ref[cut])

    def one(k, carry):
        tv_steps(f_ref, pr_ref, pc_ref, w_ref, k)
        for t in range(TILES):
            f_ref[k, t] = (-tv_weight / step_size) * w_ref[t, :WINDOW, :]
        return carry

    lax.fori_loop(0, 4, one, 0)
    for t in range(TILES):
        cut = (slice(None), slice(t * HC, (t + 1) * HC))
        product = 0.0
        for k, frame in enumerate(frames):
            video = f_ref[k, t]
            videos[k][cut] = video
            product += video * frame[(0,) + cut]
        product_ref[cut] = product


def tv_scratch(frames):
    return [
        pltpu.VMEM((WINDOW, WIDE), jnp.float32),
        pltpu.VMEM((frames, TILES, WINDOW, HC), jnp.float32),
        pltpu.VMEM((TILES, WINDOW + PAD, HC), jnp.float32),
        pltpu.VMEM((TILES, WINDOW, HC), jnp.float32),
        pltpu.VMEM((TILES, WINDOW + PAD, HC), jnp.float32),
    ]


def first_denoise(at, frames, ratios):
    window = f32(WINDOW, WIDE)
    out = pl.pallas_call(
        first_kernel,
        out_shape=(window,) * 5,
        in_specs=[SMEM] + [VMEM] * 8,
        out_specs=(VMEM,) * 5,
        scratch_shapes=tv_scratch(4),
        name="tv_first",
    )(at, *frames, *ratios)
    return out[:4], out[4]


def last_kernel(at_ref, frame_ref, video_ref, *refs):
    ratios, out_ref = refs[:4], refs[4]
    ratio_ref, f_ref, pr_ref, pc_ref, w_ref = refs[5:]
    load_ratio(at_ref, ratios, ratio_ref)
    scale = step_size / tv_weight
    pr_ref[:, :PAD, :] = jnp.zeros((TILES, PAD, HC), jnp.float32)
    for t in range(TILES):
        cut = (slice(None), slice(t * HC, (t + 1) * HC))
        f_ref[0, t] = scale * (video_ref[cut] + frame_ref[(0,) + cut] * ratio_ref[cut])
    tv_steps(f_ref, pr_ref, pc_ref, w_ref, 0)
    core = pl.multiple_of(at_ref[4], HR)
    for t in range(TILES - 1):
        out_ref[:, t * HC : (t + 1) * HC] = (-tv_weight / step_size) * w_ref[at_ref[5] + t, pl.ds(core, QUARTER), :]


def last_denoise(at, frame, video, ratios):
    return pl.pallas_call(
        last_kernel,
        out_shape=f32(QUARTER, COLS),
        in_specs=[SMEM] + [VMEM] * 6,
        out_specs=VMEM,
        scratch_shapes=tv_scratch(1),
        name="tv_last",
    )(at, frame, video, *ratios)


def join_kernel(at_ref, *refs):
    for k in range(4):
        refs[4][pl.ds(pl.multiple_of(at_ref[k], QUARTER), QUARTER), :] = refs[k][...]


def join(at, blocks):
    return pl.pallas_call(
        join_kernel,
        out_shape=f32(ROWS, COLS),
        in_specs=[SMEM] + [VMEM] * 4,
        out_specs=VMEM,
        name="join",
    )(at, *blocks)


def table(*values):
    return jnp.stack(values).astype(jnp.int32)


def per_device(measurement, masks, estimate):
    masks = masks[0]
    video = estimate[0]
    row = lax.axis_index("row")
    col = lax.axis_index("col")
    frame = lax.axis_index("frame")
    z, x = frame // 8, (frame // 2) % 4
    mine = jnp.where(col == 0, z, x)
    other = jnp.where(col == 0, x, z)

    swap = [(0, 1), (1, 0)]
    trio = (masks, video, measurement)
    c0 = jnp.where(col == 0, COLS - HC, 0)
    r0 = jnp.where(row == 0, ROWS - HR, 0)
    edge = jnp.stack([lax.dynamic_slice(a, (0, c0), (ROWS, HC)) for a in trio])
    beside = lax.ppermute(edge, "col", swap)
    strip = jnp.stack([lax.dynamic_slice(a, (r0, 0), (HR, COLS)) for a in trio])
    corner = lax.dynamic_slice(beside, (0, r0, 0), (3, HR, HC))
    strip = jnp.where(col == 0, jnp.concatenate([strip, corner], 2), jnp.concatenate([corner, strip], 2))
    below = lax.ppermute(strip, "row", swap)

    starts = [window_start((mine + turn) % 4, row) for turn in (0,) + TURNS]
    *windows, sensor = pack(table(row, col, *starts), masks, video, measurement, beside, below)
    frames = [windows[0]] + [hop(windows[1 + n], 0, turn) for n, turn in enumerate(TURNS)]

    def total(field):
        def part(turn):
            return lax.dynamic_slice_in_dim(field, (other + turn) % 4 * CHUNK, CHUNK, field.ndim - 2)

        got = part(0)
        for block in [hop(part(turn), 1, turn) for turn in TURNS]:
            got = got + block
        return got + hop(got, 2, 1)

    def spread(chunk):
        return [chunk] + [hop(chunk, 1, turn) for turn in TURNS]

    spots = [(other - turn) % 4 * CHUNK for turn in (0,) + TURNS]
    spots += [mine * QUARTER + row * HR - starts[0], col]
    at = table(*spots)
    sensor = lax.dynamic_slice_in_dim(sensor, other * CHUNK, CHUNK, 0)

    sums = total(tally(frames))
    count = sums[0]
    ratios = spread((sensor - sums[1]) / count)
    videos, product = first_denoise(at, frames, ratios)
    ratios = spread((sensor - total(product)) / count)
    blocks = []
    for n, turn in enumerate(TURNS):
        blocks.append(hop(last_denoise(at, frames[1 + n], videos[1 + n], ratios), 0, 4 - turn))
    own = last_denoise(at, frames[0], videos[0], ratios)
    places = table(*[(mine + turn) % 4 * QUARTER for turn in (0,) + TURNS])
    return join(places, [own] + blocks)[None]


def solution(mesh):
    return jax.shard_map(
        per_device,
        mesh=mesh,
        in_specs=(P("row", "col"), P("frame", "row", "col"), P("frame", "row", "col")),
        out_specs=P("frame", "row", "col"),
        check_vma=False,
    )
```

```python
import functools

import jax
import jax.numpy as jnp
from jax import lax
from jax.experimental import pallas as pl
from jax.experimental.pallas import tpu as pltpu
from jax.sharding import PartitionSpec as P

PROJ = 2
TV_ITERS = 5

tv_weight = 0.1
step_size = 0.125

ROWS = 512
COLS = 1024
QUARTER = ROWS // 4
HR = 16
HC = 128
WINDOW = QUARTER + 2 * HR
WIDE = COLS + HC
TILES = WIDE // HC
CHUNK = WINDOW // 4
MAIN = WINDOW - HR
STRIP = COLS // HC * HR
PAD = 8
TINY = 1e-35
TURNS = (1, 3, 2)


VMEM = pl.BlockSpec(memory_space=pltpu.VMEM)
SMEM = pl.BlockSpec(memory_space=pltpu.SMEM)


def f32(*shape):
    return jax.ShapeDtypeStruct(shape, jnp.float32)


def shifted(level, distance):
    pairs = []
    for frame in range(32):
        z, x, y = frame // 8, (frame // 2) % 4, frame % 2
        for core in range(2):
            tz, tx, ty = z, x, y
            if level == 2:
                ty = (y + distance) % 2
            elif (level == 0) == (core == 0):
                tz = (z + distance) % 4
            else:
                tx = (x + distance) % 4
            pairs.append((frame * 2 + core, (tz * 8 + tx * 2 + ty) * 2 + core))
    return pairs


def hop(block, level, distance):
    return lax.ppermute(block, ("frame", "col"), shifted(level, distance))


def window_start(quarter, row):
    return jnp.clip(quarter * QUARTER - HR * (1 - row), 0, ROWS - MAIN)


def strips_kernel(at_ref, masks_ref, video_ref, sensor_ref, beside_ref, below_ref, *refs):
    outs, sensor_out, all_ref = refs[:4], refs[4], refs[5]
    row = at_ref[0]
    own = pl.multiple_of(row * HR, HR)
    other = pl.multiple_of((1 - row) * ROWS, HR)
    for n, source in enumerate((masks_ref, video_ref, sensor_ref)):
        all_ref[pl.ds(own, ROWS), :COLS] = source[...]
        all_ref[pl.ds(own, ROWS), COLS:] = beside_ref[n]
        all_ref[pl.ds(other, HR), :] = below_ref[n]
        for k in range(4 if n < 2 else 1):
            start = pl.multiple_of(at_ref[1 + k], HR)
            strip = pl.multiple_of(start + (1 - row) * MAIN, HR)
            if n < 2:
                for t in range(TILES - 1):
                    outs[k][n, t * HR : (t + 1) * HR, :] = all_ref[pl.ds(strip, HR), t * HC : (t + 1) * HC]
                outs[k][n, STRIP:, :] = all_ref[pl.ds(start, WINDOW), COLS:]
            else:
                sensor_out[:MAIN, :COLS] = all_ref[pl.ds(pl.multiple_of(start + own, HR), MAIN), :COLS]
                sensor_out[MAIN:, :COLS] = all_ref[pl.ds(strip, HR), :COLS]
                sensor_out[:, COLS:] = all_ref[pl.ds(start, WINDOW), COLS:]


def cut_strips(at, masks, video, sensor, beside, below):
    return pl.pallas_call(
        strips_kernel,
        out_shape=(f32(2, STRIP + WINDOW, HC),) * 4 + (f32(WINDOW, WIDE),),
        in_specs=[SMEM] + [VMEM] * 5,
        out_specs=(VMEM,) * 5,
        scratch_shapes=[pltpu.VMEM((ROWS + HR, WIDE), jnp.float32)],
        name="strips",
    )(at, masks, video, sensor, beside, below)


def packed_parts():
    for t in range(TILES - 1):
        yield t, (slice(0, MAIN), slice(t * HC, (t + 1) * HC)), 0, (slice(0, MAIN), slice(t * HC, (t + 1) * HC))
    for t in range(TILES - 1):
        yield t, (slice(MAIN, WINDOW), slice(t * HC, (t + 1) * HC)), 1, (slice(t * HR, (t + 1) * HR), slice(None))
    yield None, (slice(0, WINDOW), slice(COLS, WIDE)), 1, (slice(STRIP, STRIP + WINDOW), slice(None))


def tiled_place(t, packed, row, col):
    if t is None:
        return (1 - col) * (TILES - 1), slice(None)
    if packed[0].start == 0:
        return col + t, pl.ds(pl.multiple_of(row * HR, HR), MAIN)
    return col + t, pl.ds(pl.multiple_of((1 - row) * MAIN, HR), HR)


def write_pieces(at_ref, whole_ref, outs):
    for k, out in enumerate(outs):
        piece = (pl.ds(pl.multiple_of(at_ref[k], PAD), CHUNK), slice(None))
        for n in range(2) if len(out.shape) == 3 else (None,):
            lead = () if n is None else (n,)
            out[lead + (slice(None), slice(None))] = whole_ref[lead + piece]


def tally_kernel(at_ref, *refs, last):
    before = refs[0] if last else None
    frames = refs[1:5] if last else refs[:4]
    outs = refs[5:9] if last else refs[4:]
    sums_ref = refs[9] if last else refs[4]
    for _, packed, source, cut in packed_parts():
        count = before[(0,) + packed] if last else 0.0
        measured = before[(1,) + packed] if last else 0.0
        for k in range(2):
            pair = frames[2 * k + source]
            masks = pair[(0,) + cut]
            count += masks * masks
            measured += masks * pair[(1,) + cut]
        sums_ref[(0,) + packed] = count
        sums_ref[(1,) + packed] = measured
    if last:
        write_pieces(at_ref, sums_ref, outs)


def tally(at, frames, before=None):
    last = before is not None
    return pl.pallas_call(
        functools.partial(tally_kernel, last=last),
        out_shape=(f32(2, CHUNK, WIDE),) * 4 if last else f32(2, WINDOW, WIDE),
        in_specs=[SMEM] + [VMEM] * (5 if last else 4),
        out_specs=(VMEM,) * 4 if last else VMEM,
        scratch_shapes=[pltpu.VMEM((2, WINDOW, WIDE), jnp.float32)] if last else [],
        name="tally_last" if last else "tally",
    )(at, *([before] if last else []), *frames)


def tv_steps(f_ref, pr_ref, pc_ref, w_ref, frame, at, rows):
    tiles, _, lanes = f_ref.shape[1:]
    lane = lax.broadcasted_iota(jnp.int32, (rows, lanes), 1)

    def dual():
        before = 0.0
        for t in range(tiles):
            pc = pc_ref[t, :rows, :]
            turned = pltpu.roll(pc, 1, 1)
            left = jnp.where(lane == 0, before, turned)
            before = turned
            pr = pr_ref[t, PAD : PAD + rows, :]
            up = pr_ref[t, PAD - 1 : PAD - 1 + rows, :]
            w_ref[t, :rows, :] = step_size * ((pr - up) + (pc - left)) - f_ref[frame, t, pl.ds(at, rows), :]
        w_ref[:, rows : rows + 1, :] = w_ref[:, rows - 1 : rows, :]

    def update(start):
        turned = pltpu.roll(w_ref[0, :rows, :], lanes - 1, 1)
        for t in range(tiles):
            w = w_ref[t, :rows, :]
            following = pltpu.roll(w_ref[t + 1, :rows, :], lanes - 1, 1) if t + 1 < tiles else w
            right = jnp.where(lane == lanes - 1, following, turned)
            turned = following
            gr = w_ref[t, 1 : rows + 1, :] - w
            gc = right - w
            s = gr * gr + gc * gc
            inv = 1.0 / (1.0 + s * lax.rsqrt(jnp.maximum(s, TINY)))
            if not start:
                gr = pr_ref[t, PAD : PAD + rows, :] + gr
                gc = pc_ref[t, :rows, :] + gc
            pr_ref[t, PAD : PAD + rows, :] = gr * inv
            pc_ref[t, :rows, :] = gc * inv

    for t in range(tiles):
        w_ref[t, :rows, :] = -f_ref[frame, t, pl.ds(at, rows), :]
    w_ref[:, rows : rows + 1, :] = w_ref[:, rows - 1 : rows, :]
    update(True)

    def iteration(_, carry):
        dual()
        update(False)
        return carry

    lax.fori_loop(1, TV_ITERS, iteration, 0)
    dual()


def load_ratio(at_ref, ratios, ratio_ref):
    for k, ratio in enumerate(ratios):
        ratio_ref[pl.ds(pl.multiple_of(at_ref[k], PAD), CHUNK), :] = ratio[...]


def first_kernel(at_ref, *refs):
    pairs, ratios, videos, products = refs[:8], refs[8:12], refs[12:16], refs[16:20]
    ratio_ref, f_ref, pr_ref, pc_ref, w_ref, product_ref = refs[20:]
    row = at_ref[8]
    col = at_ref[9]
    load_ratio(at_ref, ratios, ratio_ref)
    scale = step_size / tv_weight
    pr_ref[:, :PAD, :] = jnp.zeros((TILES, PAD, HC), jnp.float32)
    for k in range(4):
        for t, packed, source, cut in packed_parts():
            pair = pairs[2 * k + source]
            tile, rows = tiled_place(t, packed, row, col)
            f_ref[k, tile, rows, :] = scale * (pair[(1,) + cut] + pair[(0,) + cut] * ratio_ref[packed])

    def one(k, carry):
        tv_steps(f_ref, pr_ref, pc_ref, w_ref, k, 0, WINDOW)
        for t in range(TILES):
            f_ref[k, t] = (-tv_weight / step_size) * w_ref[t, :WINDOW, :]
        return carry

    lax.fori_loop(0, 4, one, 0)
    for t, packed, source, cut in packed_parts():
        tile, rows = tiled_place(t, packed, row, col)
        product = 0.0
        for k in range(4):
            product += f_ref[k, tile, rows, :] * pairs[2 * k + source][(0,) + cut]
        product_ref[packed] = product
    for k in range(4):
        videos[k][...] = f_ref[k]
    write_pieces(at_ref.at[4:8], product_ref, products)


def tv_scratch(frames):
    return [
        pltpu.VMEM((WINDOW, WIDE), jnp.float32),
        pltpu.VMEM((frames, TILES, WINDOW, HC), jnp.float32),
        pltpu.VMEM((TILES, WINDOW + PAD, HC), jnp.float32),
        pltpu.VMEM((TILES, WINDOW, HC), jnp.float32),
        pltpu.VMEM((TILES, WINDOW + PAD, HC), jnp.float32),
    ]


def first_denoise(at, pairs, ratios):
    out = pl.pallas_call(
        first_kernel,
        out_shape=(f32(TILES, WINDOW, HC),) * 4 + (f32(CHUNK, WIDE),) * 4,
        in_specs=[SMEM] + [VMEM] * 12,
        out_specs=(VMEM,) * 8,
        scratch_shapes=tv_scratch(4) + [pltpu.VMEM((WINDOW, WIDE), jnp.float32)],
        name="tv_first",
    )(at, *pairs, *ratios)
    return out[:4], out[4:]


def last_kernel(at_ref, main_ref, strip_ref, video_ref, *refs):
    ratios, out_ref = refs[:4], refs[4]
    ratio_ref, f_ref, pr_ref, pc_ref, w_ref = refs[5:]
    row = at_ref[8]
    col = at_ref[9]
    load_ratio(at_ref, ratios, ratio_ref)
    scale = step_size / tv_weight
    pr_ref[:, :PAD, :] = jnp.zeros((TILES, PAD, HC), jnp.float32)
    pair = (main_ref, strip_ref)
    for t, packed, source, cut in packed_parts():
        tile, rows = tiled_place(t, packed, row, col)
        f_ref[0, tile, rows, :] = scale * (video_ref[tile, rows, :] + pair[source][(0,) + cut] * ratio_ref[packed])
    half = pl.multiple_of(at_ref[10], PAD)
    tv_steps(f_ref, pr_ref, pc_ref, w_ref, 0, half, MAIN)
    for t in range(TILES - 1):
        out_ref[:, t * HC : (t + 1) * HC] = (-tv_weight / step_size) * w_ref[col + t, pl.ds(half, QUARTER), :]


def last_denoise(at, pair, video, ratios):
    return pl.pallas_call(
        last_kernel,
        out_shape=f32(QUARTER, COLS),
        in_specs=[SMEM] + [VMEM] * 7,
        out_specs=VMEM,
        scratch_shapes=tv_scratch(1),
        name="tv_last",
    )(at, *pair, video, *ratios)


def join_kernel(at_ref, *refs):
    blocks, out_ref, sems = refs[:4], refs[4], refs[5]
    copies = []
    for k, block in enumerate(blocks):
        place = out_ref.at[pl.ds(pl.multiple_of(at_ref[k], QUARTER), QUARTER), :]
        copies.append(pltpu.make_async_copy(block, place, sems.at[k]))
        copies[-1].start()
    for copy in copies:
        copy.wait()


def join(at, blocks):
    anywhere = pl.BlockSpec(memory_space=pl.ANY)
    return pl.pallas_call(
        join_kernel,
        out_shape=f32(ROWS, COLS),
        in_specs=[SMEM] + [anywhere] * 4,
        out_specs=anywhere,
        scratch_shapes=[pltpu.SemaphoreType.DMA((4,))],
        name="join",
    )(at, *blocks)


def table(*values):
    return jnp.stack(values).astype(jnp.int32)


def per_device(measurement, masks, estimate):
    masks = masks[0]
    video = estimate[0]
    row = lax.axis_index("row")
    col = lax.axis_index("col")
    frame = lax.axis_index("frame")
    z, x = frame // 8, (frame // 2) % 4
    mine = jnp.where(col == 0, z, x)
    other = jnp.where(col == 0, x, z)

    starts = [window_start((mine + turn) % 4, row) for turn in (0,) + TURNS]

    def main(start):
        return jnp.stack([lax.dynamic_slice_in_dim(a, start, MAIN, 0) for a in (masks, video)])

    mains = [main(starts[0])] + [hop(main(starts[1 + n]), 0, turn) for n, turn in enumerate(TURNS)]

    swap = [(0, 1), (1, 0)]
    trio = (masks, video, measurement)
    c0 = jnp.where(col == 0, COLS - HC, 0)
    r0 = jnp.where(row == 0, ROWS - HR, 0)
    edge = jnp.stack([lax.dynamic_slice(a, (0, c0), (ROWS, HC)) for a in trio])
    beside = lax.ppermute(edge, "col", swap)
    strip = jnp.stack([lax.dynamic_slice(a, (r0, 0), (HR, COLS)) for a in trio])
    corner = lax.dynamic_slice(beside, (0, r0, 0), (3, HR, HC))
    below = lax.ppermute(jnp.concatenate([strip, corner], 2), "row", swap)
    *strips, sensor = cut_strips(table(row, *starts), masks, video, measurement, beside, below)
    strips = [strips[0]] + [hop(strips[1 + n], 0, turn) for n, turn in enumerate(TURNS)]

    def total(pieces):
        got = pieces[0]
        for block in [hop(piece, 1, turn) for piece, turn in zip(pieces[1:], TURNS)]:
            got = got + block
        return got + hop(got, 2, 1)

    def spread(chunk):
        return [chunk] + [hop(chunk, 1, turn) for turn in TURNS]

    sources = [(other - turn) % 4 * CHUNK for turn in (0,) + TURNS]
    targets = [(other + turn) % 4 * CHUNK for turn in (0,) + TURNS]
    half = (mine * QUARTER - HR * (1 - row) - starts[0] + HR) // 2
    at = table(*sources, *targets, row, col, half)
    sensor = lax.dynamic_slice_in_dim(sensor, other * CHUNK, CHUNK, 0)

    pairs = [block for both in zip(mains, strips) for block in both]
    target = table(*targets)
    sums = total(tally(target, pairs[4:], tally(target, pairs[:4])))
    count = sums[0]
    ratios = spread((sensor - sums[1]) / count)
    videos, products = first_denoise(at, pairs, ratios)
    ratios = spread((sensor - total(products)) / count)
    blocks = []
    for n, turn in enumerate(TURNS):
        blocks.append(hop(last_denoise(at, pairs[2 + 2 * n : 4 + 2 * n], videos[1 + n], ratios), 0, 4 - turn))
    own = last_denoise(at, pairs[:2], videos[0], ratios)
    places = table(*[(mine + turn) % 4 * QUARTER for turn in (0,) + TURNS])
    return join(places, [own] + blocks)[None]


def solution(mesh):
    return jax.shard_map(
        per_device,
        mesh=mesh,
        in_specs=(P("row", "col"), P("frame", "row", "col"), P("frame", "row", "col")),
        out_specs=P("frame", "row", "col"),
        check_vma=False,
    )
```

```python
import functools

import jax
import jax.numpy as jnp
from jax import lax
from jax.experimental import pallas as pl
from jax.experimental.pallas import tpu as pltpu
from jax.sharding import PartitionSpec as P

PROJ = 2
TV_ITERS = 5

tv_weight = 0.1
step_size = 0.125

ROWS = 512
COLS = 1024
QUARTER = ROWS // 4
HR = 16
HC = 128
WINDOW = QUARTER + 2 * HR
WIDE = COLS + HC
TILES = WIDE // HC
CHUNK = WINDOW // 4
MAIN = WINDOW - HR
STRIP = COLS // HC * HR
PAD = 8
TINY = 1e-35
TURNS = (1, 3, 2)


VMEM = pl.BlockSpec(memory_space=pltpu.VMEM)
SMEM = pl.BlockSpec(memory_space=pltpu.SMEM)


def near(*blocks):
    return [pltpu.with_memory_space_constraint(block, pltpu.VMEM) for block in blocks]


def grant(mib):
    return pltpu.CompilerParams(vmem_limit_bytes=mib << 20)


def f32(*shape):
    return jax.ShapeDtypeStruct(shape, jnp.float32)


def shifted(level, distance):
    pairs = []
    for frame in range(32):
        z, x, y = frame // 8, (frame // 2) % 4, frame % 2
        for core in range(2):
            tz, tx, ty = z, x, y
            if level == 2:
                ty = (y + distance) % 2
            elif (level == 0) == (core == 0):
                tz = (z + distance) % 4
            else:
                tx = (x + distance) % 4
            pairs.append((frame * 2 + core, (tz * 8 + tx * 2 + ty) * 2 + core))
    return pairs


def hop(block, level, distance):
    return lax.ppermute(block, ("frame", "col"), shifted(level, distance))


def window_start(quarter, row):
    return jnp.clip(quarter * QUARTER - HR * (1 - row), 0, ROWS - MAIN)


def cut_kernel(at_ref, masks_ref, video_ref, sensor_ref, *refs):
    mains, edge_ref, strip_ref, corner_ref = refs[:4], refs[4], refs[5], refs[6]
    for k in (1, 2, 3, 0):
        rows = pl.ds(pl.multiple_of(at_ref[k], HR), MAIN)
        mains[k][0] = masks_ref[rows, :]
        mains[k][1] = video_ref[rows, :]
    rows = pl.ds(pl.multiple_of((1 - at_ref[4]) * (ROWS - HR), HR), HR)
    cols = pl.ds(pl.multiple_of((1 - at_ref[5]) * (COLS - HC), HC), HC)
    for n, source in enumerate((masks_ref, video_ref, sensor_ref)):
        edge_ref[n] = source[:, cols]
        strip_ref[n] = source[rows, :]
        corner_ref[n] = source[rows, cols]


def cut(at, masks, video, sensor):
    return pl.pallas_call(
        cut_kernel,
        out_shape=(f32(2, MAIN, COLS),) * 4 + (f32(3, ROWS, HC), f32(3, HR, COLS), f32(3, HR, HC)),
        in_specs=[SMEM] + [VMEM] * 3,
        out_specs=(VMEM,) * 7,
        name="cut",
        compiler_params=grant(24),
    )(at, masks, video, sensor)


def strips_kernel(at_ref, masks_ref, video_ref, sensor_ref, beside_ref, below_ref, corner_ref, *refs):
    outs, sensor_out, all_ref = refs[:4], refs[4], refs[5]
    row = at_ref[0]
    own = pl.multiple_of(row * HR, HR)
    other = pl.multiple_of((1 - row) * ROWS, HR)
    for n, source in enumerate((masks_ref, video_ref, sensor_ref)):
        all_ref[pl.ds(own, ROWS), :COLS] = source[...]
        all_ref[pl.ds(own, ROWS), COLS:] = beside_ref[n]
        all_ref[pl.ds(other, HR), :COLS] = below_ref[n]
        all_ref[pl.ds(other, HR), COLS:] = corner_ref[n]
        for k in range(4 if n < 2 else 1):
            start = pl.multiple_of(at_ref[1 + k], HR)
            strip = pl.multiple_of(start + (1 - row) * MAIN, HR)
            if n < 2:
                for t in range(TILES - 1):
                    outs[k][n, t * HR : (t + 1) * HR, :] = all_ref[pl.ds(strip, HR), t * HC : (t + 1) * HC]
                outs[k][n, STRIP:, :] = all_ref[pl.ds(start, WINDOW), COLS:]
            else:
                sensor_out[:MAIN, :COLS] = all_ref[pl.ds(pl.multiple_of(start + own, HR), MAIN), :COLS]
                sensor_out[MAIN:, :COLS] = all_ref[pl.ds(strip, HR), :COLS]
                sensor_out[:, COLS:] = all_ref[pl.ds(start, WINDOW), COLS:]


def cut_strips(at, masks, video, sensor, beside, below, corner):
    return pl.pallas_call(
        strips_kernel,
        out_shape=(f32(2, STRIP + WINDOW, HC),) * 4 + (f32(WINDOW, WIDE),),
        in_specs=[SMEM] + [VMEM] * 6,
        out_specs=(VMEM,) * 5,
        scratch_shapes=[pltpu.VMEM((ROWS + HR, WIDE), jnp.float32)],
        name="strips",
        compiler_params=grant(24),
    )(at, masks, video, sensor, *near(beside, below, corner))


def packed_parts():
    for t in range(TILES - 1):
        yield t, (slice(0, MAIN), slice(t * HC, (t + 1) * HC)), 0, (slice(0, MAIN), slice(t * HC, (t + 1) * HC))
    for t in range(TILES - 1):
        yield t, (slice(MAIN, WINDOW), slice(t * HC, (t + 1) * HC)), 1, (slice(t * HR, (t + 1) * HR), slice(None))
    yield None, (slice(0, WINDOW), slice(COLS, WIDE)), 1, (slice(STRIP, STRIP + WINDOW), slice(None))


def tiled_place(t, packed, row, col):
    if t is None:
        return (1 - col) * (TILES - 1), slice(None)
    if packed[0].start == 0:
        return col + t, pl.ds(pl.multiple_of(row * HR, HR), MAIN)
    return col + t, pl.ds(pl.multiple_of((1 - row) * MAIN, HR), HR)


def write_pieces(at_ref, whole_ref, outs):
    for k, out in enumerate(outs):
        piece = (pl.ds(pl.multiple_of(at_ref[k], PAD), CHUNK), slice(None))
        for n in range(2) if len(out.shape) == 3 else (None,):
            lead = () if n is None else (n,)
            out[lead + (slice(None), slice(None))] = whole_ref[lead + piece]


def tally_kernel(at_ref, *refs, last):
    before = refs[0] if last else None
    frames = refs[1:5] if last else refs[:4]
    outs = refs[5:9] if last else refs[4:]
    sums_ref = refs[9] if last else refs[4]
    for _, packed, source, cut in packed_parts():
        count = before[(0,) + packed] if last else 0.0
        measured = before[(1,) + packed] if last else 0.0
        for k in range(2):
            pair = frames[2 * k + source]
            masks = pair[(0,) + cut]
            count += masks * masks
            measured += masks * pair[(1,) + cut]
        sums_ref[(0,) + packed] = count
        sums_ref[(1,) + packed] = measured
    if last:
        write_pieces(at_ref, sums_ref, outs)


def tally(at, frames, before=None):
    last = before is not None
    return pl.pallas_call(
        functools.partial(tally_kernel, last=last),
        out_shape=(f32(2, CHUNK, WIDE),) * 4 if last else f32(2, WINDOW, WIDE),
        in_specs=[SMEM] + [VMEM] * (5 if last else 4),
        out_specs=(VMEM,) * 4 if last else VMEM,
        scratch_shapes=[pltpu.VMEM((2, WINDOW, WIDE), jnp.float32)] if last else [],
        name="tally_last" if last else "tally",
        compiler_params=grant(20),
    )(at, *near(*([before] if last else []), *frames))


def tv_steps(f_ref, pr_ref, pc_ref, w_ref, frame, at, rows):
    tiles, _, lanes = f_ref.shape[1:]
    lane = lax.broadcasted_iota(jnp.int32, (rows, lanes), 1)

    def dual():
        before = 0.0
        for t in range(tiles):
            pc = pc_ref[t, :rows, :]
            turned = pltpu.roll(pc, 1, 1)
            left = jnp.where(lane == 0, before, turned)
            before = turned
            pr = pr_ref[t, PAD : PAD + rows, :]
            up = pr_ref[t, PAD - 1 : PAD - 1 + rows, :]
            w_ref[t, :rows, :] = step_size * ((pr - up) + (pc - left)) - f_ref[frame, t, pl.ds(at, rows), :]
        w_ref[:, rows : rows + 1, :] = w_ref[:, rows - 1 : rows, :]

    def update(start):
        turned = pltpu.roll(w_ref[0, :rows, :], lanes - 1, 1)
        for t in range(tiles):
            w = w_ref[t, :rows, :]
            following = pltpu.roll(w_ref[t + 1, :rows, :], lanes - 1, 1) if t + 1 < tiles else w
            right = jnp.where(lane == lanes - 1, following, turned)
            turned = following
            gr = w_ref[t, 1 : rows + 1, :] - w
            gc = right - w
            s = gr * gr + gc * gc
            inv = 1.0 / (1.0 + s * lax.rsqrt(jnp.maximum(s, TINY)))
            if not start:
                gr = pr_ref[t, PAD : PAD + rows, :] + gr
                gc = pc_ref[t, :rows, :] + gc
            pr_ref[t, PAD : PAD + rows, :] = gr * inv
            pc_ref[t, :rows, :] = gc * inv

    for t in range(tiles):
        w_ref[t, :rows, :] = -f_ref[frame, t, pl.ds(at, rows), :]
    w_ref[:, rows : rows + 1, :] = w_ref[:, rows - 1 : rows, :]
    update(True)

    def iteration(_, carry):
        dual()
        update(False)
        return carry

    lax.fori_loop(1, TV_ITERS, iteration, 0)
    dual()


def load_ratio(at_ref, ratios, ratio_ref):
    for k, ratio in enumerate(ratios):
        ratio_ref[pl.ds(pl.multiple_of(at_ref[k], PAD), CHUNK), :] = ratio[...]


def first_kernel(at_ref, *refs):
    pairs, ratios, videos, products = refs[:8], refs[8:12], refs[12:16], refs[16:20]
    ratio_ref, f_ref, pr_ref, pc_ref, w_ref, product_ref = refs[20:]
    row = at_ref[8]
    col = at_ref[9]
    load_ratio(at_ref, ratios, ratio_ref)
    scale = step_size / tv_weight
    pr_ref[:, :PAD, :] = jnp.zeros((TILES, PAD, HC), jnp.float32)
    for k in range(4):
        for t, packed, source, cut in packed_parts():
            pair = pairs[2 * k + source]
            tile, rows = tiled_place(t, packed, row, col)
            f_ref[k, tile, rows, :] = scale * (pair[(1,) + cut] + pair[(0,) + cut] * ratio_ref[packed])

    def one(k, carry):
        tv_steps(f_ref, pr_ref, pc_ref, w_ref, k, 0, WINDOW)
        for t in range(TILES):
            f_ref[k, t] = (-tv_weight / step_size) * w_ref[t, :WINDOW, :]
        return carry

    lax.fori_loop(0, 4, one, 0)
    for t, packed, source, cut in packed_parts():
        tile, rows = tiled_place(t, packed, row, col)
        product = 0.0
        for k in range(4):
            product += f_ref[k, tile, rows, :] * pairs[2 * k + source][(0,) + cut]
        product_ref[packed] = product
    for k in range(4):
        videos[k][...] = f_ref[k]
    write_pieces(at_ref.at[4:8], product_ref, products)


def tv_scratch(frames):
    return [
        pltpu.VMEM((WINDOW, WIDE), jnp.float32),
        pltpu.VMEM((frames, TILES, WINDOW, HC), jnp.float32),
        pltpu.VMEM((TILES, WINDOW + PAD, HC), jnp.float32),
        pltpu.VMEM((TILES, WINDOW, HC), jnp.float32),
        pltpu.VMEM((TILES, WINDOW + PAD, HC), jnp.float32),
    ]


def first_denoise(at, pairs, ratios):
    out = pl.pallas_call(
        first_kernel,
        out_shape=(f32(TILES, WINDOW, HC),) * 4 + (f32(CHUNK, WIDE),) * 4,
        in_specs=[SMEM] + [VMEM] * 12,
        out_specs=(VMEM,) * 8,
        scratch_shapes=tv_scratch(4) + [pltpu.VMEM((WINDOW, WIDE), jnp.float32)],
        name="tv_first",
        compiler_params=grant(36),
    )(at, *near(*pairs, *ratios))
    return out[:4], out[4:]


def last_kernel(at_ref, main_ref, strip_ref, video_ref, *refs):
    ratios, out_ref = refs[:4], refs[4]
    ratio_ref, f_ref, pr_ref, pc_ref, w_ref = refs[5:]
    row = at_ref[8]
    col = at_ref[9]
    load_ratio(at_ref, ratios, ratio_ref)
    scale = step_size / tv_weight
    pr_ref[:, :PAD, :] = jnp.zeros((TILES, PAD, HC), jnp.float32)
    pair = (main_ref, strip_ref)
    for t, packed, source, cut in packed_parts():
        tile, rows = tiled_place(t, packed, row, col)
        f_ref[0, tile, rows, :] = scale * (video_ref[tile, rows, :] + pair[source][(0,) + cut] * ratio_ref[packed])
    half = pl.multiple_of(at_ref[10], PAD)
    tv_steps(f_ref, pr_ref, pc_ref, w_ref, 0, half, MAIN)
    for t in range(TILES - 1):
        out_ref[:, t * HC : (t + 1) * HC] = (-tv_weight / step_size) * w_ref[col + t, pl.ds(half, QUARTER), :]


def last_denoise(at, pair, video, ratios):
    return pl.pallas_call(
        last_kernel,
        out_shape=f32(QUARTER, COLS),
        in_specs=[SMEM] + [VMEM] * 7,
        out_specs=VMEM,
        scratch_shapes=tv_scratch(1),
        name="tv_last",
        compiler_params=grant(16),
    )(at, *near(*pair, video, *ratios))


def join_kernel(at_ref, *refs):
    for k in range(4):
        refs[4][pl.ds(pl.multiple_of(at_ref[k], QUARTER), QUARTER), :] = refs[k][...]


def join(at, blocks):
    return pl.pallas_call(
        join_kernel,
        out_shape=f32(ROWS, COLS),
        in_specs=[SMEM] + [VMEM] * 4,
        out_specs=VMEM,
        name="join",
        compiler_params=grant(16),
    )(at, *near(*blocks))


def table(*values):
    return jnp.stack(values).astype(jnp.int32)


def per_device(measurement, masks, estimate):
    masks = masks[0]
    video = estimate[0]
    row = lax.axis_index("row")
    col = lax.axis_index("col")
    frame = lax.axis_index("frame")
    z, x = frame // 8, (frame // 2) % 4
    mine = jnp.where(col == 0, z, x)
    other = jnp.where(col == 0, x, z)

    starts = [window_start((mine + turn) % 4, row) for turn in (0,) + TURNS]

    mains = cut(table(*starts, row, col), masks, video, measurement)
    mains, (edge, strip, corner) = list(mains[:4]), mains[4:]
    mains = [mains[0]] + [hop(mains[1 + n], 0, turn) for n, turn in enumerate(TURNS)]

    swap = [(0, 1), (1, 0)]
    beside = lax.ppermute(edge, "col", swap)
    below = lax.ppermute(strip, "row", swap)
    corner = lax.ppermute(corner, ("row", "col"), [(0, 3), (3, 0), (1, 2), (2, 1)])
    *strips, sensor = cut_strips(table(row, *starts), masks, video, measurement, beside, below, corner)
    strips = [strips[0]] + [hop(strips[1 + n], 0, turn) for n, turn in enumerate(TURNS)]

    def total(pieces):
        got = pieces[0]
        for block in [hop(piece, 1, turn) for piece, turn in zip(pieces[1:], TURNS)]:
            got = got + block
        return got + hop(got, 2, 1)

    def spread(chunk):
        return [chunk] + [hop(chunk, 1, turn) for turn in TURNS]

    sources = [(other - turn) % 4 * CHUNK for turn in (0,) + TURNS]
    targets = [(other + turn) % 4 * CHUNK for turn in (0,) + TURNS]
    half = (mine * QUARTER - HR * (1 - row) - starts[0] + HR) // 2
    at = table(*sources, *targets, row, col, half)
    sensor = lax.dynamic_slice_in_dim(sensor, other * CHUNK, CHUNK, 0)

    pairs = [block for both in zip(mains, strips) for block in both]
    target = table(*targets)
    sums = total(tally(target, pairs[4:], tally(target, pairs[:4])))
    count = sums[0]
    ratios = spread((sensor - sums[1]) / count)
    videos, products = first_denoise(at, pairs, ratios)
    ratios = spread((sensor - total(products)) / count)
    blocks = []
    for n, turn in enumerate(TURNS):
        blocks.append(hop(last_denoise(at, pairs[2 + 2 * n : 4 + 2 * n], videos[1 + n], ratios), 0, 4 - turn))
    own = last_denoise(at, pairs[:2], videos[0], ratios)
    places = table(*[(mine + turn) % 4 * QUARTER for turn in (0,) + TURNS])
    return join(places, [own] + blocks)[None]


def solution(mesh):
    return jax.shard_map(
        per_device,
        mesh=mesh,
        in_specs=(P("row", "col"), P("frame", "row", "col"), P("frame", "row", "col")),
        out_specs=P("frame", "row", "col"),
        check_vma=False,
    )
```

```python
import functools

import jax
import jax.numpy as jnp
from jax import lax
from jax.experimental import pallas as pl
from jax.experimental.pallas import tpu as pltpu
from jax.sharding import PartitionSpec as P

PROJ = 2
TV_ITERS = 5

tv_weight = 0.1
step_size = 0.125

ROWS = 512
COLS = 1024
QUARTER = ROWS // 4
HR = 16
HC = 128
WINDOW = QUARTER + 2 * HR
WIDE = COLS + HC
TILES = WIDE // HC
CHUNK = WINDOW // 4
MAIN = WINDOW - HR
STRIP = COLS // HC * HR
PAD = 8
TINY = 1e-35
TURNS = (1, 3, 2)

ROW, COL, START, STRIP_AT, OUTSIDE, SOURCE, TARGET, HALF, PLACE = 0, 1, 2, 6, 10, 14, 18, 22, 23


VMEM = pl.BlockSpec(memory_space=pltpu.VMEM)
HBM = pl.BlockSpec(memory_space=pltpu.HBM)
SMEM = pl.BlockSpec(memory_space=pltpu.SMEM)


def near(*blocks):
    return [pltpu.with_memory_space_constraint(block, pltpu.VMEM) for block in blocks]


def grant(mib):
    return pltpu.CompilerParams(vmem_limit_bytes=mib << 20)


def f32(*shape):
    return jax.ShapeDtypeStruct(shape, jnp.float32)


def shifted(level, distance):
    pairs = []
    for frame in range(32):
        z, x, y = frame // 8, (frame // 2) % 4, frame % 2
        for core in range(2):
            tz, tx, ty = z, x, y
            if level == 2:
                ty = (y + distance) % 2
            elif (level == 0) == (core == 0):
                tz = (z + distance) % 4
            else:
                tx = (x + distance) % 4
            pairs.append((frame * 2 + core, (tz * 8 + tx * 2 + ty) * 2 + core))
    return pairs


def hop(block, level, distance):
    return lax.ppermute(block, ("frame", "col"), shifted(level, distance))


def window_start(quarter, row):
    return jnp.clip(quarter * QUARTER - HR * (1 - row), 0, ROWS - MAIN)


def cut_kernel(at_ref, masks_ref, video_ref, sensor_ref, *refs):
    mains, strips_ref, main_ref, edge_ref, end_ref, corner_ref, sems = refs[:4], *refs[4:]
    copies = []

    def copy(source, target):
        copies.append(pltpu.make_async_copy(source, target, sems.at[len(copies)]))
        copies[-1].start()

    for k in (1, 2, 3, 0):
        rows = pl.ds(pl.multiple_of(at_ref[START + k], HR), MAIN)
        copy(masks_ref.at[rows, :], mains[k].at[0])
        copy(video_ref.at[rows, :], mains[k].at[1])
    rows = pl.ds(pl.multiple_of((1 - at_ref[ROW]) * (ROWS - HR), HR), HR)
    cols = pl.ds(pl.multiple_of((1 - at_ref[COL]) * (COLS - HC), HC), HC)
    for n, source in enumerate((masks_ref, video_ref, sensor_ref)):
        copy(source.at[:, cols], edge_ref.at[n])
        copy(source.at[rows, :], end_ref.at[n])
        copy(source.at[rows, cols], corner_ref.at[n])
        for k in range(4 if n < 2 else 1):
            copy(source.at[pl.ds(pl.multiple_of(at_ref[STRIP_AT + k], HR), HR), :], strips_ref.at[4 * n + k])
    copy(sensor_ref.at[pl.ds(pl.multiple_of(at_ref[START], HR), MAIN), :], main_ref)
    for one in copies:
        one.wait()


def cut(at, masks, video, sensor):
    return pl.pallas_call(
        cut_kernel,
        out_shape=(f32(2, MAIN, COLS),) * 4 + (f32(9, HR, COLS), f32(MAIN, COLS), f32(3, ROWS, HC), f32(3, HR, COLS), f32(3, HR, HC)),
        in_specs=[SMEM] + [HBM] * 3,
        out_specs=(VMEM,) * 9,
        scratch_shapes=[pltpu.SemaphoreType.DMA((27,))],
        name="cut",
        compiler_params=grant(24),
    )(at, masks, video, sensor)


def strips_kernel(at_ref, strips_ref, main_ref, beside_ref, below_ref, corner_ref, *refs):
    outs, sensor_ref, cols_ref, packed_ref = refs[:4], *refs[4:]
    row = at_ref[ROW]
    own = pl.multiple_of(row * HR, HR)
    other = pl.multiple_of((1 - row) * ROWS, HR)
    for n in range(3):
        cols_ref[pl.ds(own, ROWS), :] = beside_ref[n]
        cols_ref[pl.ds(other, HR), :] = corner_ref[n]
        for k in range(4 if n < 2 else 1):
            start = pl.multiple_of(at_ref[START + k], HR)
            strip = jnp.where(at_ref[OUTSIDE + k] == 1, below_ref[n], strips_ref[4 * n + k])
            if n < 2:
                for t in range(TILES - 1):
                    outs[k][n, t * HR : (t + 1) * HR, :] = strip[:, t * HC : (t + 1) * HC]
                outs[k][n, STRIP:, :] = cols_ref[pl.ds(start, WINDOW), :]
            else:
                packed_ref[:MAIN, :COLS] = main_ref[...]
                packed_ref[MAIN:, :COLS] = strip
                packed_ref[:, COLS:] = cols_ref[pl.ds(start, WINDOW), :]
    sensor_ref[...] = packed_ref[pl.ds(pl.multiple_of(at_ref[TARGET], PAD), CHUNK), :]


def cut_strips(at, *blocks):
    return pl.pallas_call(
        strips_kernel,
        out_shape=(f32(2, STRIP + WINDOW, HC),) * 4 + (f32(CHUNK, WIDE),),
        in_specs=[SMEM] + [VMEM] * 5,
        out_specs=(VMEM,) * 5,
        scratch_shapes=[pltpu.VMEM((ROWS + HR, HC), jnp.float32), pltpu.VMEM((WINDOW, WIDE), jnp.float32)],
        name="strips",
        compiler_params=grant(20),
    )(at, *near(*blocks))


def sum_kernel(*refs):
    refs[-1][...] = (refs[0][...] + refs[1][...]) + (refs[2][...] + refs[3][...])


def summed(blocks):
    return pl.pallas_call(
        sum_kernel,
        out_shape=f32(*blocks[0].shape),
        in_specs=[VMEM] * 4,
        out_specs=VMEM,
        name="summed",
        compiler_params=grant(8),
    )(*near(*blocks))


def first_ratio_kernel(mine_ref, other_ref, sensor_ref, ratio_ref, count_ref):
    count = mine_ref[0] + other_ref[0]
    count_ref[...] = count
    ratio_ref[...] = (sensor_ref[...] - (mine_ref[1] + other_ref[1])) / count


def ratio_kernel(mine_ref, other_ref, sensor_ref, count_ref, ratio_ref):
    ratio_ref[...] = (sensor_ref[...] - (mine_ref[...] + other_ref[...])) / count_ref[...]


def ratio_of(first, *blocks):
    chunk = f32(CHUNK, WIDE)
    return pl.pallas_call(
        first_ratio_kernel if first else ratio_kernel,
        out_shape=(chunk, chunk) if first else chunk,
        in_specs=[VMEM] * len(blocks),
        out_specs=(VMEM, VMEM) if first else VMEM,
        name="first_ratio" if first else "ratio",
        compiler_params=grant(8),
    )(*near(*blocks))


def packed_parts():
    for t in range(TILES - 1):
        yield t, (slice(0, MAIN), slice(t * HC, (t + 1) * HC)), 0, (slice(0, MAIN), slice(t * HC, (t + 1) * HC))
    for t in range(TILES - 1):
        yield t, (slice(MAIN, WINDOW), slice(t * HC, (t + 1) * HC)), 1, (slice(t * HR, (t + 1) * HR), slice(None))
    yield None, (slice(0, WINDOW), slice(COLS, WIDE)), 1, (slice(STRIP, STRIP + WINDOW), slice(None))


def tiled_place(t, packed, row, col):
    if t is None:
        return (1 - col) * (TILES - 1), slice(None)
    if packed[0].start == 0:
        return col + t, pl.ds(pl.multiple_of(row * HR, HR), MAIN)
    return col + t, pl.ds(pl.multiple_of((1 - row) * MAIN, HR), HR)


def write_pieces(at_ref, whole_ref, outs):
    for k, out in enumerate(outs):
        piece = (pl.ds(pl.multiple_of(at_ref[TARGET + k], PAD), CHUNK), slice(None))
        for n in range(2) if len(out.shape) == 3 else (None,):
            lead = () if n is None else (n,)
            out[lead + (slice(None), slice(None))] = whole_ref[lead + piece]


def tally_kernel(at_ref, *refs, last):
    before = refs[0] if last else None
    frames = refs[1:5] if last else refs[:4]
    outs = refs[5:9] if last else refs[4:]
    sums_ref = refs[9] if last else refs[4]
    for _, packed, source, cut in packed_parts():
        count = before[(0,) + packed] if last else 0.0
        measured = before[(1,) + packed] if last else 0.0
        for k in range(2):
            pair = frames[2 * k + source]
            masks = pair[(0,) + cut]
            count += masks * masks
            measured += masks * pair[(1,) + cut]
        sums_ref[(0,) + packed] = count
        sums_ref[(1,) + packed] = measured
    if last:
        write_pieces(at_ref, sums_ref, outs)


def tally(at, frames, before=None):
    last = before is not None
    return pl.pallas_call(
        functools.partial(tally_kernel, last=last),
        out_shape=(f32(2, CHUNK, WIDE),) * 4 if last else f32(2, WINDOW, WIDE),
        in_specs=[SMEM] + [VMEM] * (5 if last else 4),
        out_specs=(VMEM,) * 4 if last else VMEM,
        scratch_shapes=[pltpu.VMEM((2, WINDOW, WIDE), jnp.float32)] if last else [],
        name="tally_last" if last else "tally",
        compiler_params=grant(20),
    )(at, *near(*([before] if last else []), *frames))


def tv_steps(f_ref, pr_ref, pc_ref, w_ref, frame, at, rows):
    tiles, _, lanes = f_ref.shape[1:]
    lane = lax.broadcasted_iota(jnp.int32, (rows, lanes), 1)

    def dual():
        before = 0.0
        for t in range(tiles):
            pc = pc_ref[t, :rows, :]
            turned = pltpu.roll(pc, 1, 1)
            left = jnp.where(lane == 0, before, turned)
            before = turned
            pr = pr_ref[t, PAD : PAD + rows, :]
            up = pr_ref[t, PAD - 1 : PAD - 1 + rows, :]
            w_ref[t, :rows, :] = step_size * ((pr - up) + (pc - left)) - f_ref[frame, t, pl.ds(at, rows), :]
        w_ref[:, rows : rows + 1, :] = w_ref[:, rows - 1 : rows, :]

    def update(start):
        turned = pltpu.roll(w_ref[0, :rows, :], lanes - 1, 1)
        for t in range(tiles):
            w = w_ref[t, :rows, :]
            following = pltpu.roll(w_ref[t + 1, :rows, :], lanes - 1, 1) if t + 1 < tiles else w
            right = jnp.where(lane == lanes - 1, following, turned)
            turned = following
            gr = w_ref[t, 1 : rows + 1, :] - w
            gc = right - w
            s = gr * gr + gc * gc
            inv = 1.0 / (1.0 + s * lax.rsqrt(jnp.maximum(s, TINY)))
            if not start:
                gr = pr_ref[t, PAD : PAD + rows, :] + gr
                gc = pc_ref[t, :rows, :] + gc
            pr_ref[t, PAD : PAD + rows, :] = gr * inv
            pc_ref[t, :rows, :] = gc * inv

    for t in range(tiles):
        w_ref[t, :rows, :] = -f_ref[frame, t, pl.ds(at, rows), :]
    w_ref[:, rows : rows + 1, :] = w_ref[:, rows - 1 : rows, :]
    update(True)

    def iteration(_, carry):
        dual()
        update(False)
        return carry

    lax.fori_loop(1, TV_ITERS, iteration, 0)
    dual()


def load_ratio(at_ref, ratios, ratio_ref):
    for k, ratio in enumerate(ratios):
        ratio_ref[pl.ds(pl.multiple_of(at_ref[SOURCE + k], PAD), CHUNK), :] = ratio[...]


def first_kernel(at_ref, *refs):
    pairs, ratios, videos, products = refs[:8], refs[8:12], refs[12:16], refs[16:20]
    ratio_ref, f_ref, pr_ref, pc_ref, w_ref, product_ref = refs[20:]
    row = at_ref[ROW]
    col = at_ref[COL]
    load_ratio(at_ref, ratios, ratio_ref)
    scale = step_size / tv_weight
    pr_ref[:, :PAD, :] = jnp.zeros((TILES, PAD, HC), jnp.float32)
    for k in range(4):
        for t, packed, source, cut in packed_parts():
            pair = pairs[2 * k + source]
            tile, rows = tiled_place(t, packed, row, col)
            f_ref[k, tile, rows, :] = scale * (pair[(1,) + cut] + pair[(0,) + cut] * ratio_ref[packed])

    def one(k, carry):
        tv_steps(f_ref, pr_ref, pc_ref, w_ref, k, 0, WINDOW)
        for t in range(TILES):
            f_ref[k, t] = (-tv_weight / step_size) * w_ref[t, :WINDOW, :]
        return carry

    lax.fori_loop(0, 4, one, 0)
    for t, packed, source, cut in packed_parts():
        tile, rows = tiled_place(t, packed, row, col)
        product = 0.0
        for k in range(4):
            product += f_ref[k, tile, rows, :] * pairs[2 * k + source][(0,) + cut]
        product_ref[packed] = product
    for k in range(4):
        videos[k][...] = f_ref[k]
    write_pieces(at_ref, product_ref, products)


def tv_scratch(frames):
    return [
        pltpu.VMEM((WINDOW, WIDE), jnp.float32),
        pltpu.VMEM((frames, TILES, WINDOW, HC), jnp.float32),
        pltpu.VMEM((TILES, WINDOW + PAD, HC), jnp.float32),
        pltpu.VMEM((TILES, WINDOW, HC), jnp.float32),
        pltpu.VMEM((TILES, WINDOW + PAD, HC), jnp.float32),
    ]


def first_denoise(at, pairs, ratios):
    out = pl.pallas_call(
        first_kernel,
        out_shape=(f32(TILES, WINDOW, HC),) * 4 + (f32(CHUNK, WIDE),) * 4,
        in_specs=[SMEM] + [VMEM] * 12,
        out_specs=(VMEM,) * 8,
        scratch_shapes=tv_scratch(4) + [pltpu.VMEM((WINDOW, WIDE), jnp.float32)],
        name="tv_first",
        compiler_params=grant(36),
    )(at, *near(*pairs, *ratios))
    return out[:4], out[4:]


def last_kernel(at_ref, main_ref, strip_ref, video_ref, *refs):
    ratios, out_ref = refs[:4], refs[4]
    ratio_ref, f_ref, pr_ref, pc_ref, w_ref = refs[5:]
    row = at_ref[ROW]
    col = at_ref[COL]
    load_ratio(at_ref, ratios, ratio_ref)
    scale = step_size / tv_weight
    pr_ref[:, :PAD, :] = jnp.zeros((TILES, PAD, HC), jnp.float32)
    pair = (main_ref, strip_ref)
    for t, packed, source, cut in packed_parts():
        tile, rows = tiled_place(t, packed, row, col)
        f_ref[0, tile, rows, :] = scale * (video_ref[tile, rows, :] + pair[source][(0,) + cut] * ratio_ref[packed])
    half = pl.multiple_of(at_ref[HALF], PAD)
    tv_steps(f_ref, pr_ref, pc_ref, w_ref, 0, half, MAIN)
    for t in range(TILES - 1):
        out_ref[:, t * HC : (t + 1) * HC] = (-tv_weight / step_size) * w_ref[col + t, pl.ds(half, QUARTER), :]


def last_denoise(at, pair, video, ratios):
    return pl.pallas_call(
        last_kernel,
        out_shape=f32(QUARTER, COLS),
        in_specs=[SMEM] + [VMEM] * 7,
        out_specs=VMEM,
        scratch_shapes=tv_scratch(1),
        name="tv_last",
        compiler_params=grant(16),
    )(at, *near(*pair, video, *ratios))


def join_kernel(at_ref, *refs):
    blocks, out_ref, sems = refs[:4], refs[4], refs[5]
    copies = []
    for k, block in enumerate(blocks):
        place = out_ref.at[pl.ds(pl.multiple_of(at_ref[PLACE + k], QUARTER), QUARTER), :]
        copies.append(pltpu.make_async_copy(block, place, sems.at[k]))
        copies[-1].start()
    for one in copies:
        one.wait()


def join(at, blocks):
    return pl.pallas_call(
        join_kernel,
        out_shape=f32(ROWS, COLS),
        in_specs=[SMEM] + [VMEM] * 4,
        out_specs=HBM,
        scratch_shapes=[pltpu.SemaphoreType.DMA((4,))],
        name="join",
        compiler_params=grant(8),
    )(at, *near(*blocks))


def table(*values):
    return jnp.stack([jnp.asarray(value, jnp.int32) for value in values])


def per_device(measurement, masks, estimate):
    masks = masks[0]
    video = estimate[0]
    row = lax.axis_index("row")
    col = lax.axis_index("col")
    frame = lax.axis_index("frame")
    z, x = frame // 8, (frame // 2) % 4
    mine = jnp.where(col == 0, z, x)
    other = jnp.where(col == 0, x, z)

    starts = [window_start((mine + turn) % 4, row) for turn in (0,) + TURNS]
    strip_at = [jnp.where(row == 0, jnp.minimum(start + MAIN, ROWS - HR), jnp.maximum(start - HR, 0)) for start in starts]
    outside = [start == (ROWS - MAIN) * (1 - row) for start in starts]
    sources = [(other - turn) % 4 * CHUNK for turn in (0,) + TURNS]
    targets = [(other + turn) % 4 * CHUNK for turn in (0,) + TURNS]
    half = (mine * QUARTER - HR * (1 - row) - starts[0] + HR) // 2
    places = [(mine + turn) % 4 * QUARTER for turn in (0,) + TURNS]
    at = table(row, col, *starts, *strip_at, *outside, *sources, *targets, half, *places)

    *mains, strips, sensor, edge, end, corner = cut(at, masks, video, measurement)
    mains = [mains[0]] + [hop(mains[1 + n], 0, turn) for n, turn in enumerate(TURNS)]
    swap = [(0, 1), (1, 0)]
    beside = lax.ppermute(edge, "col", swap)
    below = lax.ppermute(end, "row", swap)
    corner = lax.ppermute(corner, ("row", "col"), [(0, 3), (3, 0), (1, 2), (2, 1)])
    *strips, sensor = cut_strips(at, strips, sensor, beside, below, corner)
    strips = [strips[0]] + [hop(strips[1 + n], 0, turn) for n, turn in enumerate(TURNS)]
    pairs = [block for both in zip(mains, strips) for block in both]

    def total(pieces):
        got = summed([pieces[0]] + [hop(piece, 1, turn) for piece, turn in zip(pieces[1:], TURNS)])
        return got, hop(got, 2, 1)

    def spread(chunk):
        return [chunk] + [hop(chunk, 1, turn) for turn in TURNS]

    sums = total(tally(at, pairs[4:], tally(at, pairs[:4])))
    ratio, count = ratio_of(True, *sums, sensor)
    videos, products = first_denoise(at, pairs, spread(ratio))
    ratios = spread(ratio_of(False, *total(products), sensor, count))
    blocks = []
    for n, turn in enumerate(TURNS):
        blocks.append(hop(last_denoise(at, pairs[2 + 2 * n : 4 + 2 * n], videos[1 + n], ratios), 0, 4 - turn))
    own = last_denoise(at, pairs[:2], videos[0], ratios)
    return join(at, [own] + blocks)[None]


def solution(mesh):
    return jax.shard_map(
        per_device,
        mesh=mesh,
        in_specs=(P("row", "col"), P("frame", "row", "col"), P("frame", "row", "col")),
        out_specs=P("frame", "row", "col"),
        check_vma=False,
    )
```

```python
import functools

import jax
import jax.numpy as jnp
from jax import lax
from jax.experimental import pallas as pl
from jax.experimental.pallas import tpu as pltpu
from jax.sharding import PartitionSpec as P

PROJ = 2
TV_ITERS = 5

tv_weight = 0.1
step_size = 0.125

ROWS = 512
COLS = 1024
QUARTER = ROWS // 4
HR = 16
HC = 128
WINDOW = QUARTER + 2 * HR
WIDE = COLS + HC
TILES = WIDE // HC
CHUNK = WINDOW // 4
MAIN = WINDOW - HR
STRIP = COLS // HC * HR
PAD = 8
TINY = 1e-35
TURNS = (1, 3, 2)

ROW, COL, START, STRIP_AT, OUTSIDE, SOURCE, TARGET, HALF, PLACE = 0, 1, 2, 6, 10, 14, 18, 22, 23


VMEM = pl.BlockSpec(memory_space=pltpu.VMEM)
HBM = pl.BlockSpec(memory_space=pltpu.HBM)
SMEM = pl.BlockSpec(memory_space=pltpu.SMEM)


def near(*blocks):
    return [pltpu.with_memory_space_constraint(block, pltpu.VMEM) for block in blocks]


def grant(mib):
    return pltpu.CompilerParams(vmem_limit_bytes=mib << 20)


def f32(*shape):
    return jax.ShapeDtypeStruct(shape, jnp.float32)


def shifted(level, distance):
    pairs = []
    for frame in range(32):
        z, x, y = frame // 8, (frame // 2) % 4, frame % 2
        for core in range(2):
            tz, tx, ty = z, x, y
            if level == 2:
                ty = (y + distance) % 2
            elif (level == 0) == (core == 0):
                tz = (z + distance) % 4
            else:
                tx = (x + distance) % 4
            pairs.append((frame * 2 + core, (tz * 8 + tx * 2 + ty) * 2 + core))
    return pairs


def hop(block, level, distance):
    return lax.ppermute(block, ("frame", "col"), shifted(level, distance))


def window_start(quarter, row):
    return jnp.clip(quarter * QUARTER - HR * (1 - row), 0, ROWS - MAIN)


def cut_kernel(at_ref, masks_ref, video_ref, sensor_ref, *refs):
    mains, strips_ref, main_ref, edge_ref, end_ref, corner_ref, sems = refs[:4], *refs[4:]
    copies = []

    def copy(source, target):
        copies.append(pltpu.make_async_copy(source, target, sems.at[len(copies)]))
        copies[-1].start()

    for k in (1, 2, 3, 0):
        rows = pl.ds(pl.multiple_of(at_ref[START + k], HR), MAIN)
        copy(masks_ref.at[rows, :], mains[k].at[0])
        copy(video_ref.at[rows, :], mains[k].at[1])
    rows = pl.ds(pl.multiple_of((1 - at_ref[ROW]) * (ROWS - HR), HR), HR)
    cols = pl.ds(pl.multiple_of((1 - at_ref[COL]) * (COLS - HC), HC), HC)
    for n, source in enumerate((masks_ref, video_ref, sensor_ref)):
        copy(source.at[:, cols], edge_ref.at[n])
        copy(source.at[rows, :], end_ref.at[n])
        copy(source.at[rows, cols], corner_ref.at[n])
        for k in range(4 if n < 2 else 1):
            copy(source.at[pl.ds(pl.multiple_of(at_ref[STRIP_AT + k], HR), HR), :], strips_ref.at[4 * n + k])
    copy(sensor_ref.at[pl.ds(pl.multiple_of(at_ref[START], HR), MAIN), :], main_ref)
    for one in copies:
        one.wait()


def cut(at, masks, video, sensor):
    return pl.pallas_call(
        cut_kernel,
        out_shape=(f32(2, MAIN, COLS),) * 4 + (f32(9, HR, COLS), f32(MAIN, COLS), f32(3, ROWS, HC), f32(3, HR, COLS), f32(3, HR, HC)),
        in_specs=[SMEM] + [HBM] * 3,
        out_specs=(VMEM,) * 9,
        scratch_shapes=[pltpu.SemaphoreType.DMA((27,))],
        name="cut",
        compiler_params=grant(24),
    )(at, *[pltpu.with_memory_space_constraint(a, pltpu.HBM) for a in (masks, video, sensor)])


def strips_kernel(at_ref, strips_ref, main_ref, beside_ref, below_ref, corner_ref, *refs):
    outs, sensor_ref, cols_ref, packed_ref = refs[:4], *refs[4:]
    row = at_ref[ROW]
    own = pl.multiple_of(row * HR, HR)
    other = pl.multiple_of((1 - row) * ROWS, HR)
    for n in range(3):
        cols_ref[pl.ds(own, ROWS), :] = beside_ref[n]
        cols_ref[pl.ds(other, HR), :] = corner_ref[n]
        for k in range(4 if n < 2 else 1):
            start = pl.multiple_of(at_ref[START + k], HR)
            strip = jnp.where(at_ref[OUTSIDE + k] == 1, below_ref[n], strips_ref[4 * n + k])
            if n < 2:
                for t in range(TILES - 1):
                    outs[k][n, t * HR : (t + 1) * HR, :] = strip[:, t * HC : (t + 1) * HC]
                outs[k][n, STRIP:, :] = cols_ref[pl.ds(start, WINDOW), :]
            else:
                packed_ref[:MAIN, :COLS] = main_ref[...]
                packed_ref[MAIN:, :COLS] = strip
                packed_ref[:, COLS:] = cols_ref[pl.ds(start, WINDOW), :]
    sensor_ref[...] = packed_ref[pl.ds(pl.multiple_of(at_ref[TARGET], PAD), CHUNK), :]


def cut_strips(at, *blocks):
    return pl.pallas_call(
        strips_kernel,
        out_shape=(f32(2, STRIP + WINDOW, HC),) * 4 + (f32(CHUNK, WIDE),),
        in_specs=[SMEM] + [VMEM] * 5,
        out_specs=(VMEM,) * 5,
        scratch_shapes=[pltpu.VMEM((ROWS + HR, HC), jnp.float32), pltpu.VMEM((WINDOW, WIDE), jnp.float32)],
        name="strips",
        compiler_params=grant(20),
    )(at, *near(*blocks))


def sum_kernel(*refs):
    refs[-1][...] = (refs[0][...] + refs[1][...]) + (refs[2][...] + refs[3][...])


def summed(blocks):
    return pl.pallas_call(
        sum_kernel,
        out_shape=f32(*blocks[0].shape),
        in_specs=[VMEM] * 4,
        out_specs=VMEM,
        name="summed",
        compiler_params=grant(8),
    )(*near(*blocks))


def first_ratio_kernel(mine_ref, other_ref, sensor_ref, ratio_ref, count_ref):
    count = mine_ref[0] + other_ref[0]
    count_ref[...] = count
    ratio_ref[...] = (sensor_ref[...] - (mine_ref[1] + other_ref[1])) / count


def ratio_kernel(mine_ref, other_ref, sensor_ref, count_ref, ratio_ref):
    ratio_ref[...] = (sensor_ref[...] - (mine_ref[...] + other_ref[...])) / count_ref[...]


def ratio_of(first, *blocks):
    chunk = f32(CHUNK, WIDE)
    return pl.pallas_call(
        first_ratio_kernel if first else ratio_kernel,
        out_shape=(chunk, chunk) if first else chunk,
        in_specs=[VMEM] * len(blocks),
        out_specs=(VMEM, VMEM) if first else VMEM,
        name="first_ratio" if first else "ratio",
        compiler_params=grant(8),
    )(*near(*blocks))


def packed_parts():
    for t in range(TILES - 1):
        yield t, (slice(0, MAIN), slice(t * HC, (t + 1) * HC)), 0, (slice(0, MAIN), slice(t * HC, (t + 1) * HC))
    for t in range(TILES - 1):
        yield t, (slice(MAIN, WINDOW), slice(t * HC, (t + 1) * HC)), 1, (slice(t * HR, (t + 1) * HR), slice(None))
    yield None, (slice(0, WINDOW), slice(COLS, WIDE)), 1, (slice(STRIP, STRIP + WINDOW), slice(None))


def tiled_place(t, packed, row, col):
    if t is None:
        return (1 - col) * (TILES - 1), slice(None)
    if packed[0].start == 0:
        return col + t, pl.ds(pl.multiple_of(row * HR, HR), MAIN)
    return col + t, pl.ds(pl.multiple_of((1 - row) * MAIN, HR), HR)


def write_pieces(at_ref, whole_ref, outs):
    for k, out in enumerate(outs):
        piece = (pl.ds(pl.multiple_of(at_ref[TARGET + k], PAD), CHUNK), slice(None))
        for n in range(2) if len(out.shape) == 3 else (None,):
            lead = () if n is None else (n,)
            out[lead + (slice(None), slice(None))] = whole_ref[lead + piece]


def tally_kernel(at_ref, *refs, last):
    before = refs[0] if last else None
    frames = refs[1:5] if last else refs[:4]
    outs = refs[5:9] if last else refs[4:]
    sums_ref = refs[9] if last else refs[4]
    for _, packed, source, cut in packed_parts():
        count = before[(0,) + packed] if last else 0.0
        measured = before[(1,) + packed] if last else 0.0
        for k in range(2):
            pair = frames[2 * k + source]
            masks = pair[(0,) + cut]
            count += masks * masks
            measured += masks * pair[(1,) + cut]
        sums_ref[(0,) + packed] = count
        sums_ref[(1,) + packed] = measured
    if last:
        write_pieces(at_ref, sums_ref, outs)


def tally(at, frames, before=None):
    last = before is not None
    return pl.pallas_call(
        functools.partial(tally_kernel, last=last),
        out_shape=(f32(2, CHUNK, WIDE),) * 4 if last else f32(2, WINDOW, WIDE),
        in_specs=[SMEM] + [VMEM] * (5 if last else 4),
        out_specs=(VMEM,) * 4 if last else VMEM,
        scratch_shapes=[pltpu.VMEM((2, WINDOW, WIDE), jnp.float32)] if last else [],
        name="tally_last" if last else "tally",
        compiler_params=grant(20),
    )(at, *near(*([before] if last else []), *frames))


def tv_steps(f_ref, pr_ref, pc_ref, w_ref, frame, at, rows):
    tiles, _, lanes = f_ref.shape[1:]
    lane = lax.broadcasted_iota(jnp.int32, (rows, lanes), 1)

    def dual():
        before = 0.0
        for t in range(tiles):
            pc = pc_ref[t, :rows, :]
            turned = pltpu.roll(pc, 1, 1)
            left = jnp.where(lane == 0, before, turned)
            before = turned
            pr = pr_ref[t, PAD : PAD + rows, :]
            up = pr_ref[t, PAD - 1 : PAD - 1 + rows, :]
            w_ref[t, :rows, :] = step_size * ((pr - up) + (pc - left)) - f_ref[frame, t, pl.ds(at, rows), :]
        w_ref[:, rows : rows + 1, :] = w_ref[:, rows - 1 : rows, :]

    def update(start):
        turned = pltpu.roll(w_ref[0, :rows, :], lanes - 1, 1)
        for t in range(tiles):
            w = w_ref[t, :rows, :]
            following = pltpu.roll(w_ref[t + 1, :rows, :], lanes - 1, 1) if t + 1 < tiles else w
            right = jnp.where(lane == lanes - 1, following, turned)
            turned = following
            gr = w_ref[t, 1 : rows + 1, :] - w
            gc = right - w
            s = gr * gr + gc * gc
            inv = 1.0 / (1.0 + s * lax.rsqrt(jnp.maximum(s, TINY)))
            if not start:
                gr = pr_ref[t, PAD : PAD + rows, :] + gr
                gc = pc_ref[t, :rows, :] + gc
            pr_ref[t, PAD : PAD + rows, :] = gr * inv
            pc_ref[t, :rows, :] = gc * inv

    for t in range(tiles):
        w_ref[t, :rows, :] = -f_ref[frame, t, pl.ds(at, rows), :]
    w_ref[:, rows : rows + 1, :] = w_ref[:, rows - 1 : rows, :]
    update(True)

    def iteration(_, carry):
        dual()
        update(False)
        return carry

    lax.fori_loop(1, TV_ITERS, iteration, 0)
    dual()


def load_ratio(at_ref, ratios, ratio_ref):
    for k, ratio in enumerate(ratios):
        ratio_ref[pl.ds(pl.multiple_of(at_ref[SOURCE + k], PAD), CHUNK), :] = ratio[...]


def first_kernel(at_ref, *refs):
    pairs, ratios, videos, products = refs[:8], refs[8:12], refs[12:16], refs[16:20]
    ratio_ref, f_ref, pr_ref, pc_ref, w_ref, product_ref = refs[20:]
    row = at_ref[ROW]
    col = at_ref[COL]
    load_ratio(at_ref, ratios, ratio_ref)
    scale = step_size / tv_weight
    pr_ref[:, :PAD, :] = jnp.zeros((TILES, PAD, HC), jnp.float32)
    for k in range(4):
        for t, packed, source, cut in packed_parts():
            pair = pairs[2 * k + source]
            tile, rows = tiled_place(t, packed, row, col)
            f_ref[k, tile, rows, :] = scale * (pair[(1,) + cut] + pair[(0,) + cut] * ratio_ref[packed])

    def one(k, carry):
        tv_steps(f_ref, pr_ref, pc_ref, w_ref, k, 0, WINDOW)
        for t in range(TILES):
            f_ref[k, t] = (-tv_weight / step_size) * w_ref[t, :WINDOW, :]
        return carry

    lax.fori_loop(0, 4, one, 0)
    for t, packed, source, cut in packed_parts():
        tile, rows = tiled_place(t, packed, row, col)
        product = 0.0
        for k in range(4):
            product += f_ref[k, tile, rows, :] * pairs[2 * k + source][(0,) + cut]
        product_ref[packed] = product
    for k in range(4):
        videos[k][...] = f_ref[k]
    write_pieces(at_ref, product_ref, products)


def tv_scratch(frames):
    return [
        pltpu.VMEM((WINDOW, WIDE), jnp.float32),
        pltpu.VMEM((frames, TILES, WINDOW, HC), jnp.float32),
        pltpu.VMEM((TILES, WINDOW + PAD, HC), jnp.float32),
        pltpu.VMEM((TILES, WINDOW, HC), jnp.float32),
        pltpu.VMEM((TILES, WINDOW + PAD, HC), jnp.float32),
    ]


def first_denoise(at, pairs, ratios):
    out = pl.pallas_call(
        first_kernel,
        out_shape=(f32(TILES, WINDOW, HC),) * 4 + (f32(CHUNK, WIDE),) * 4,
        in_specs=[SMEM] + [VMEM] * 12,
        out_specs=(VMEM,) * 8,
        scratch_shapes=tv_scratch(4) + [pltpu.VMEM((WINDOW, WIDE), jnp.float32)],
        name="tv_first",
        compiler_params=grant(36),
    )(at, *near(*pairs, *ratios))
    return out[:4], out[4:]


def last_kernel(at_ref, main_ref, strip_ref, video_ref, *refs):
    ratios, out_ref = refs[:4], refs[4]
    ratio_ref, f_ref, pr_ref, pc_ref, w_ref = refs[5:]
    row = at_ref[ROW]
    col = at_ref[COL]
    load_ratio(at_ref, ratios, ratio_ref)
    scale = step_size / tv_weight
    pr_ref[:, :PAD, :] = jnp.zeros((TILES, PAD, HC), jnp.float32)
    pair = (main_ref, strip_ref)
    for t, packed, source, cut in packed_parts():
        tile, rows = tiled_place(t, packed, row, col)
        f_ref[0, tile, rows, :] = scale * (video_ref[tile, rows, :] + pair[source][(0,) + cut] * ratio_ref[packed])
    half = pl.multiple_of(at_ref[HALF], PAD)
    tv_steps(f_ref, pr_ref, pc_ref, w_ref, 0, half, MAIN)
    for t in range(TILES - 1):
        out_ref[:, t * HC : (t + 1) * HC] = (-tv_weight / step_size) * w_ref[col + t, pl.ds(half, QUARTER), :]


def last_denoise(at, pair, video, ratios):
    return pl.pallas_call(
        last_kernel,
        out_shape=f32(QUARTER, COLS),
        in_specs=[SMEM] + [VMEM] * 7,
        out_specs=VMEM,
        scratch_shapes=tv_scratch(1),
        name="tv_last",
        compiler_params=grant(16),
    )(at, *near(*pair, video, *ratios))


def join_kernel(at_ref, *refs, spots):
    out_ref, sems = refs[-2:]
    copies = []
    for n, k in enumerate(spots):
        place = out_ref.at[pl.ds(pl.multiple_of(at_ref[PLACE + k], QUARTER), QUARTER), :]
        copies.append(pltpu.make_async_copy(refs[n], place, sems.at[n]))
        copies[-1].start()
    for one in copies:
        one.wait()


def join(at, blocks, spots, whole=None):
    count = len(blocks)
    return pl.pallas_call(
        functools.partial(join_kernel, spots=spots),
        out_shape=f32(ROWS, COLS),
        in_specs=[SMEM] + [VMEM] * count + ([] if whole is None else [HBM]),
        out_specs=HBM,
        scratch_shapes=[pltpu.SemaphoreType.DMA((count,))],
        input_output_aliases={} if whole is None else {1 + count: 0},
        name="join",
        compiler_params=grant(8),
    )(at, *near(*blocks), *([] if whole is None else [whole]))


def table(*values):
    return jnp.stack([jnp.asarray(value, jnp.int32) for value in values])


def per_device(measurement, masks, estimate):
    masks = masks[0]
    video = estimate[0]
    row = lax.axis_index("row")
    col = lax.axis_index("col")
    frame = lax.axis_index("frame")
    z, x = frame // 8, (frame // 2) % 4
    mine = jnp.where(col == 0, z, x)
    other = jnp.where(col == 0, x, z)

    starts = [window_start((mine + turn) % 4, row) for turn in (0,) + TURNS]
    strip_at = [jnp.where(row == 0, jnp.minimum(start + MAIN, ROWS - HR), jnp.maximum(start - HR, 0)) for start in starts]
    outside = [start == (ROWS - MAIN) * (1 - row) for start in starts]
    sources = [(other - turn) % 4 * CHUNK for turn in (0,) + TURNS]
    targets = [(other + turn) % 4 * CHUNK for turn in (0,) + TURNS]
    half = (mine * QUARTER - HR * (1 - row) - starts[0] + HR) // 2
    places = [(mine + turn) % 4 * QUARTER for turn in (0,) + TURNS]
    at = table(row, col, *starts, *strip_at, *outside, *sources, *targets, half, *places)

    *mains, strips, sensor, edge, end, corner = cut(at, masks, video, measurement)
    mains = [mains[0]] + [hop(mains[1 + n], 0, turn) for n, turn in enumerate(TURNS)]
    swap = [(0, 1), (1, 0)]
    beside = lax.ppermute(edge, "col", swap)
    below = lax.ppermute(end, "row", swap)
    corner = lax.ppermute(corner, ("row", "col"), [(0, 3), (3, 0), (1, 2), (2, 1)])
    *strips, sensor = cut_strips(at, strips, sensor, beside, below, corner)
    strips = [strips[0]] + [hop(strips[1 + n], 0, turn) for n, turn in enumerate(TURNS)]
    pairs = [block for both in zip(mains, strips) for block in both]

    def total(pieces):
        got = summed([pieces[0]] + [hop(piece, 1, turn) for piece, turn in zip(pieces[1:], TURNS)])
        return got, hop(got, 2, 1)

    def spread(chunk):
        return [chunk] + [hop(chunk, 1, turn) for turn in TURNS]

    sums = total(tally(at, pairs[4:], tally(at, pairs[:4])))
    ratio, count = ratio_of(True, *sums, sensor)
    videos, products = first_denoise(at, pairs, spread(ratio))
    ratios = spread(ratio_of(False, *total(products), sensor, count))
    blocks = []
    for n in (2, 0, 1):
        blocks.append(hop(last_denoise(at, pairs[2 + 2 * n : 4 + 2 * n], videos[1 + n], ratios), 0, 4 - TURNS[n]))
    own = last_denoise(at, pairs[:2], videos[0], ratios)
    whole = join(at, [own, blocks[0], blocks[1]], (0, 3, 1))
    return join(at, blocks[2:], (2,), whole)[None]


def solution(mesh):
    return jax.shard_map(
        per_device,
        mesh=mesh,
        in_specs=(P("row", "col"), P("frame", "row", "col"), P("frame", "row", "col")),
        out_specs=P("frame", "row", "col"),
        check_vma=False,
    )
```

```python
import functools

import jax
import jax.numpy as jnp
from jax import lax
from jax.experimental import pallas as pl
from jax.experimental.pallas import tpu as pltpu
from jax.sharding import PartitionSpec as P

PROJ = 2
TV_ITERS = 5

tv_weight = 0.1
step_size = 0.125

ROWS = 512
COLS = 1024
QUARTER = ROWS // 4
HR = 16
HC = 128
WINDOW = QUARTER + 2 * HR
TILES = COLS // HC + 1
MAIN = WINDOW - HR
STRIP = COLS // HC * HR
SIDE = 2 * HR
PACKED = COLS // HC * WINDOW + SIDE
CHUNK = PACKED // 4
PAD = 8
TINY = 1e-35
TURNS = (1, 3, 2)

ROW, COL, START, STRIP_AT, OUTSIDE, SOURCE, TARGET, HALF, PLACE = 0, 1, 2, 6, 10, 14, 18, 22, 23


VMEM = pl.BlockSpec(memory_space=pltpu.VMEM)
HBM = pl.BlockSpec(memory_space=pltpu.HBM)
SMEM = pl.BlockSpec(memory_space=pltpu.SMEM)


TURNED = pltpu.VMEM((HC, 2 * HC), jnp.float32)


def near(*blocks):
    return [pltpu.with_memory_space_constraint(block, pltpu.VMEM) for block in blocks]


def grant(mib):
    return pltpu.CompilerParams(vmem_limit_bytes=mib << 20)


def f32(*shape):
    return jax.ShapeDtypeStruct(shape, jnp.float32)


def shifted(level, distance):
    pairs = []
    for frame in range(32):
        z, x, y = frame // 8, (frame // 2) % 4, frame % 2
        for core in range(2):
            tz, tx, ty = z, x, y
            if level == 2:
                ty = (y + distance) % 2
            elif (level == 0) == (core == 0):
                tz = (z + distance) % 4
            else:
                tx = (x + distance) % 4
            pairs.append((frame * 2 + core, (tz * 8 + tx * 2 + ty) * 2 + core))
    return pairs


def hop(block, level, distance):
    return lax.ppermute(block, ("frame", "col"), shifted(level, distance))


def window_start(quarter, row):
    return jnp.clip(quarter * QUARTER - HR * (1 - row), 0, ROWS - MAIN)


def cut_kernel(at_ref, masks_ref, video_ref, sensor_ref, *refs):
    mains, strips_ref, main_ref, edge_ref, end_ref, corner_ref, sems = refs[:4], *refs[4:]
    copies = []

    def copy(source, target):
        copies.append(pltpu.make_async_copy(source, target, sems.at[len(copies)]))
        copies[-1].start()

    for k in (1, 2, 3, 0):
        rows = pl.ds(pl.multiple_of(at_ref[START + k], HR), MAIN)
        copy(masks_ref.at[rows, :], mains[k].at[0])
        copy(video_ref.at[rows, :], mains[k].at[1])
    rows = pl.ds(pl.multiple_of((1 - at_ref[ROW]) * (ROWS - HR), HR), HR)
    cols = pl.ds(pl.multiple_of((1 - at_ref[COL]) * (COLS - HC), HC), HC)
    for n, source in enumerate((masks_ref, video_ref, sensor_ref)):
        copy(source.at[:, cols], edge_ref.at[n])
        copy(source.at[rows, :], end_ref.at[n])
        copy(source.at[rows, cols], corner_ref.at[n])
        for k in range(4 if n < 2 else 1):
            copy(source.at[pl.ds(pl.multiple_of(at_ref[STRIP_AT + k], HR), HR), :], strips_ref.at[4 * n + k])
    copy(sensor_ref.at[pl.ds(pl.multiple_of(at_ref[START], HR), MAIN), :], main_ref)
    for one in copies:
        one.wait()


def cut(at, masks, video, sensor):
    return pl.pallas_call(
        cut_kernel,
        out_shape=(f32(2, MAIN, COLS),) * 4 + (f32(9, HR, COLS), f32(MAIN, COLS), f32(3, ROWS, HC), f32(3, HR, COLS), f32(3, HR, HC)),
        in_specs=[SMEM] + [HBM] * 3,
        out_specs=(VMEM,) * 9,
        scratch_shapes=[pltpu.SemaphoreType.DMA((27,))],
        name="cut",
        compiler_params=grant(24),
    )(at, *[pltpu.with_memory_space_constraint(a, pltpu.HBM) for a in (masks, video, sensor)])


def side_rows(col):
    return pl.ds(pl.multiple_of(col * (HC - HR), HR), HR)


def turn_side(rows, turned_ref, col):
    turned_ref[:, :HC] = rows[:HC].T
    turned_ref[:, HC:] = rows[HC:].T
    side = side_rows(col)
    return turned_ref[side, :HC], turned_ref[side, HC:]


def halo_tile(side, turned_ref, col):
    turned_ref[side_rows(col), :HC] = side[:HR]
    turned_ref[side_rows(col), HC:] = side[HR:]
    return turned_ref[:, :HC].T, turned_ref[:, HC:].T[: WINDOW - HC]


def strips_kernel(at_ref, strips_ref, main_ref, beside_ref, below_ref, corner_ref, *refs):
    outs, sensor_ref, cols_ref, packed_ref, turned_ref = refs[:4], *refs[4:]
    row = at_ref[ROW]
    own = pl.multiple_of(row * HR, HR)
    other = pl.multiple_of((1 - row) * ROWS, HR)
    cols_ref[ROWS + HR :, :] = jnp.zeros((2 * HC - WINDOW, HC), jnp.float32)
    for n in range(3):
        cols_ref[pl.ds(own, ROWS), :] = beside_ref[n]
        cols_ref[pl.ds(other, HR), :] = corner_ref[n]
        for k in range(4 if n < 2 else 1):
            start = pl.multiple_of(at_ref[START + k], HR)
            strip = jnp.where(at_ref[OUTSIDE + k] == 1, below_ref[n], strips_ref[4 * n + k])
            upper, lower = turn_side(cols_ref[pl.ds(start, 2 * HC), :], turned_ref, at_ref[COL])
            target, base = (outs[k].at[n], 0) if n < 2 else (packed_ref, MAIN * (TILES - 1))
            for t in range(TILES - 1):
                if n == 2:
                    target[t * MAIN : (t + 1) * MAIN, :] = main_ref[:, t * HC : (t + 1) * HC]
                target[base + t * HR : base + (t + 1) * HR, :] = strip[:, t * HC : (t + 1) * HC]
            target[base + STRIP : base + STRIP + HR, :] = upper
            target[base + STRIP + HR : base + STRIP + SIDE, :] = lower
    sensor_ref[...] = packed_ref[pl.ds(pl.multiple_of(at_ref[TARGET], PAD), CHUNK), :]


def cut_strips(at, *blocks):
    return pl.pallas_call(
        strips_kernel,
        out_shape=(f32(2, STRIP + SIDE, HC),) * 4 + (f32(CHUNK, HC),),
        in_specs=[SMEM] + [VMEM] * 5,
        out_specs=(VMEM,) * 5,
        scratch_shapes=[pltpu.VMEM((ROWS + HR + 2 * HC - WINDOW, HC), jnp.float32), pltpu.VMEM((PACKED, HC), jnp.float32), TURNED],
        name="strips",
        compiler_params=grant(20),
    )(at, *near(*blocks))


def sum_kernel(*refs):
    refs[-1][...] = (refs[0][...] + refs[1][...]) + (refs[2][...] + refs[3][...])


def summed(blocks):
    return pl.pallas_call(
        sum_kernel,
        out_shape=f32(*blocks[0].shape),
        in_specs=[VMEM] * 4,
        out_specs=VMEM,
        name="summed",
        compiler_params=grant(8),
    )(*near(*blocks))


def first_ratio_kernel(mine_ref, other_ref, sensor_ref, ratio_ref, count_ref):
    count = mine_ref[0] + other_ref[0]
    count_ref[...] = count
    ratio_ref[...] = (sensor_ref[...] - (mine_ref[1] + other_ref[1])) / count


def ratio_kernel(mine_ref, other_ref, sensor_ref, count_ref, ratio_ref):
    ratio_ref[...] = (sensor_ref[...] - (mine_ref[...] + other_ref[...])) / count_ref[...]


def ratio_of(first, *blocks):
    chunk = f32(CHUNK, HC)
    return pl.pallas_call(
        first_ratio_kernel if first else ratio_kernel,
        out_shape=(chunk, chunk) if first else chunk,
        in_specs=[VMEM] * len(blocks),
        out_specs=(VMEM, VMEM) if first else VMEM,
        name="first_ratio" if first else "ratio",
        compiler_params=grant(8),
    )(*near(*blocks))


def packed_parts():
    base = MAIN * (TILES - 1)
    for t in range(TILES - 1):
        yield t, slice(t * MAIN, (t + 1) * MAIN), 0, (slice(0, MAIN), slice(t * HC, (t + 1) * HC))
    for t in range(TILES - 1):
        yield t, slice(base + t * HR, base + (t + 1) * HR), 1, (slice(t * HR, (t + 1) * HR), slice(None))
    yield None, slice(base + STRIP, PACKED), 1, (slice(STRIP, STRIP + SIDE), slice(None))


def tiled_place(t, source, row, col):
    if source == 0:
        return col + t, pl.ds(pl.multiple_of(row * HR, HR), MAIN)
    return col + t, pl.ds(pl.multiple_of((1 - row) * MAIN, HR), HR)


def write_pieces(at_ref, whole_ref, outs):
    for k, out in enumerate(outs):
        piece = (pl.ds(pl.multiple_of(at_ref[TARGET + k], PAD), CHUNK), slice(None))
        for n in range(2) if len(out.shape) == 3 else (None,):
            lead = () if n is None else (n,)
            out[lead + (slice(None), slice(None))] = whole_ref[lead + piece]


def tally_kernel(at_ref, *refs, last):
    before = refs[0] if last else None
    frames = refs[1:5] if last else refs[:4]
    outs = refs[5:9] if last else refs[4:]
    sums_ref = refs[9] if last else refs[4]
    for _, packed, source, cut in packed_parts():
        count = before[0, packed, :] if last else 0.0
        measured = before[1, packed, :] if last else 0.0
        for k in range(2):
            pair = frames[2 * k + source]
            masks = pair[(0,) + cut]
            count += masks * masks
            measured += masks * pair[(1,) + cut]
        sums_ref[0, packed, :] = count
        sums_ref[1, packed, :] = measured
    if last:
        write_pieces(at_ref, sums_ref, outs)


def tally(at, frames, before=None):
    last = before is not None
    return pl.pallas_call(
        functools.partial(tally_kernel, last=last),
        out_shape=(f32(2, CHUNK, HC),) * 4 if last else f32(2, PACKED, HC),
        in_specs=[SMEM] + [VMEM] * (5 if last else 4),
        out_specs=(VMEM,) * 4 if last else VMEM,
        scratch_shapes=[pltpu.VMEM((2, PACKED, HC), jnp.float32)] if last else [],
        name="tally_last" if last else "tally",
        compiler_params=grant(20),
    )(at, *near(*([before] if last else []), *frames))


def tv_steps(f_ref, pr_ref, pc_ref, w_ref, frame, at, rows):
    tiles, _, lanes = f_ref.shape[1:]
    lane = lax.broadcasted_iota(jnp.int32, (rows, lanes), 1)

    def dual():
        before = 0.0
        for t in range(tiles):
            pc = pc_ref[t, :rows, :]
            turned = pltpu.roll(pc, 1, 1)
            left = jnp.where(lane == 0, before, turned)
            before = turned
            pr = pr_ref[t, PAD : PAD + rows, :]
            up = pr_ref[t, PAD - 1 : PAD - 1 + rows, :]
            w_ref[t, :rows, :] = step_size * ((pr - up) + (pc - left)) - f_ref[frame, t, pl.ds(at, rows), :]
        w_ref[:, rows : rows + 1, :] = w_ref[:, rows - 1 : rows, :]

    def update(start):
        turned = pltpu.roll(w_ref[0, :rows, :], lanes - 1, 1)
        for t in range(tiles):
            w = w_ref[t, :rows, :]
            following = pltpu.roll(w_ref[t + 1, :rows, :], lanes - 1, 1) if t + 1 < tiles else w
            right = jnp.where(lane == lanes - 1, following, turned)
            turned = following
            gr = w_ref[t, 1 : rows + 1, :] - w
            gc = right - w
            s = gr * gr + gc * gc
            inv = 1.0 / (1.0 + s * lax.rsqrt(jnp.maximum(s, TINY)))
            if not start:
                gr = pr_ref[t, PAD : PAD + rows, :] + gr
                gc = pc_ref[t, :rows, :] + gc
            pr_ref[t, PAD : PAD + rows, :] = gr * inv
            pc_ref[t, :rows, :] = gc * inv

    for t in range(tiles):
        w_ref[t, :rows, :] = -f_ref[frame, t, pl.ds(at, rows), :]
    w_ref[:, rows : rows + 1, :] = w_ref[:, rows - 1 : rows, :]
    update(True)

    def iteration(_, carry):
        dual()
        update(False)
        return carry

    lax.fori_loop(1, TV_ITERS, iteration, 0)
    dual()


def load_ratio(at_ref, ratios, ratio_ref):
    for k, ratio in enumerate(ratios):
        ratio_ref[pl.ds(pl.multiple_of(at_ref[SOURCE + k], PAD), CHUNK), :] = ratio[...]


def first_kernel(at_ref, *refs):
    pairs, ratios, videos, products = refs[:8], refs[8:12], refs[12:16], refs[16:20]
    ratio_ref, f_ref, pr_ref, pc_ref, w_ref, turned_ref, product_ref, rows_ref = refs[20:]
    row = at_ref[ROW]
    col = at_ref[COL]
    halo = (1 - col) * (TILES - 1)
    load_ratio(at_ref, ratios, ratio_ref)
    turned_ref[...] = jnp.zeros((HC, 2 * HC), jnp.float32)
    scale = step_size / tv_weight
    pr_ref[:, :PAD, :] = jnp.zeros((TILES, PAD, HC), jnp.float32)
    for k in range(4):
        for t, packed, source, cut in packed_parts():
            pair = pairs[2 * k + source]
            noisy = scale * (pair[(1,) + cut] + pair[(0,) + cut] * ratio_ref[packed, :])
            if t is None:
                f_ref[k, halo, :HC, :], f_ref[k, halo, HC:, :] = halo_tile(noisy, turned_ref, col)
            else:
                tile, rows = tiled_place(t, source, row, col)
                f_ref[k, tile, rows, :] = noisy

    def one(k, carry):
        tv_steps(f_ref, pr_ref, pc_ref, w_ref, k, 0, WINDOW)
        for t in range(TILES):
            f_ref[k, t] = (-tv_weight / step_size) * w_ref[t, :WINDOW, :]
        return carry

    lax.fori_loop(0, 4, one, 0)
    rows_ref[WINDOW:, :] = jnp.zeros((2 * HC - WINDOW, HC), jnp.float32)
    for t, packed, source, cut in packed_parts():
        product = 0.0
        for k in range(4):
            if t is None:
                rows_ref[:WINDOW, :] = f_ref[k, halo]
                video = jnp.concatenate(turn_side(rows_ref[...], turned_ref, col), 0)
            else:
                tile, rows = tiled_place(t, source, row, col)
                video = f_ref[k, tile, rows, :]
            product += video * pairs[2 * k + source][(0,) + cut]
        product_ref[packed, :] = product
    for k in range(4):
        videos[k][...] = f_ref[k]
    write_pieces(at_ref, product_ref, products)


def tv_scratch(frames):
    return [
        pltpu.VMEM((PACKED, HC), jnp.float32),
        pltpu.VMEM((frames, TILES, WINDOW, HC), jnp.float32),
        pltpu.VMEM((TILES, WINDOW + PAD, HC), jnp.float32),
        pltpu.VMEM((TILES, WINDOW, HC), jnp.float32),
        pltpu.VMEM((TILES, WINDOW + PAD, HC), jnp.float32),
        TURNED,
    ]


def first_denoise(at, pairs, ratios):
    out = pl.pallas_call(
        first_kernel,
        out_shape=(f32(TILES, WINDOW, HC),) * 4 + (f32(CHUNK, HC),) * 4,
        in_specs=[SMEM] + [VMEM] * 12,
        out_specs=(VMEM,) * 8,
        scratch_shapes=tv_scratch(4) + [pltpu.VMEM((PACKED, HC), jnp.float32), pltpu.VMEM((2 * HC, HC), jnp.float32)],
        name="tv_first",
        compiler_params=grant(36),
    )(at, *near(*pairs, *ratios))
    return out[:4], out[4:]


def last_kernel(at_ref, main_ref, strip_ref, video_ref, *refs):
    ratios, out_ref = refs[:4], refs[4]
    ratio_ref, f_ref, pr_ref, pc_ref, w_ref, turned_ref = refs[5:]
    row = at_ref[ROW]
    col = at_ref[COL]
    halo = (1 - col) * (TILES - 1)
    load_ratio(at_ref, ratios, ratio_ref)
    turned_ref[...] = jnp.zeros((HC, 2 * HC), jnp.float32)
    scale = step_size / tv_weight
    pr_ref[:, :PAD, :] = jnp.zeros((TILES, PAD, HC), jnp.float32)
    pair = (main_ref, strip_ref)
    for t, packed, source, cut in packed_parts():
        change = pair[source][(0,) + cut] * ratio_ref[packed, :]
        if t is None:
            upper, lower = halo_tile(change, turned_ref, col)
            f_ref[0, halo, :HC, :] = scale * (video_ref[halo, :HC, :] + upper)
            f_ref[0, halo, HC:, :] = scale * (video_ref[halo, HC:, :] + lower)
        else:
            tile, rows = tiled_place(t, source, row, col)
            f_ref[0, tile, rows, :] = scale * (video_ref[tile, rows, :] + change)
    half = pl.multiple_of(at_ref[HALF], PAD)
    tv_steps(f_ref, pr_ref, pc_ref, w_ref, 0, half, MAIN)
    for t in range(TILES - 1):
        out_ref[:, t * HC : (t + 1) * HC] = (-tv_weight / step_size) * w_ref[col + t, pl.ds(half, QUARTER), :]


def last_denoise(at, pair, video, ratios):
    return pl.pallas_call(
        last_kernel,
        out_shape=f32(QUARTER, COLS),
        in_specs=[SMEM] + [VMEM] * 7,
        out_specs=VMEM,
        scratch_shapes=tv_scratch(1),
        name="tv_last",
        compiler_params=grant(16),
    )(at, *near(*pair, video, *ratios))


def join_kernel(at_ref, *refs):
    blocks, out_ref, sems = refs[:4], refs[4], refs[5]
    copies = []
    for k, block in enumerate(blocks):
        place = out_ref.at[pl.ds(pl.multiple_of(at_ref[PLACE + k], QUARTER), QUARTER), :]
        copies.append(pltpu.make_async_copy(block, place, sems.at[k]))
        copies[-1].start()
    for one in copies:
        one.wait()


def join(at, blocks):
    return pl.pallas_call(
        join_kernel,
        out_shape=f32(ROWS, COLS),
        in_specs=[SMEM] + [VMEM] * 4,
        out_specs=HBM,
        scratch_shapes=[pltpu.SemaphoreType.DMA((4,))],
        name="join",
        compiler_params=grant(8),
    )(at, *near(*blocks))


def table(*values):
    return jnp.stack([jnp.asarray(value, jnp.int32) for value in values])


def per_device(measurement, masks, estimate):
    masks = masks[0]
    video = estimate[0]
    row = lax.axis_index("row")
    col = lax.axis_index("col")
    frame = lax.axis_index("frame")
    z, x = frame // 8, (frame // 2) % 4
    mine = jnp.where(col == 0, z, x)
    other = jnp.where(col == 0, x, z)

    starts = [window_start((mine + turn) % 4, row) for turn in (0,) + TURNS]
    strip_at = [jnp.where(row == 0, jnp.minimum(start + MAIN, ROWS - HR), jnp.maximum(start - HR, 0)) for start in starts]
    outside = [start == (ROWS - MAIN) * (1 - row) for start in starts]
    sources = [(other - turn) % 4 * CHUNK for turn in (0,) + TURNS]
    targets = [(other + turn) % 4 * CHUNK for turn in (0,) + TURNS]
    half = (mine * QUARTER - HR * (1 - row) - starts[0] + HR) // 2
    places = [(mine + turn) % 4 * QUARTER for turn in (0,) + TURNS]
    at = table(row, col, *starts, *strip_at, *outside, *sources, *targets, half, *places)

    *mains, strips, sensor, edge, end, corner = cut(at, masks, video, measurement)
    mains = [mains[0]] + [hop(mains[1 + n], 0, turn) for n, turn in enumerate(TURNS)]
    swap = [(0, 1), (1, 0)]
    beside = lax.ppermute(edge, "col", swap)
    below = lax.ppermute(end, "row", swap)
    corner = lax.ppermute(corner, ("row", "col"), [(0, 3), (3, 0), (1, 2), (2, 1)])
    *strips, sensor = cut_strips(at, strips, sensor, beside, below, corner)
    strips = [strips[0]] + [hop(strips[1 + n], 0, turn) for n, turn in enumerate(TURNS)]
    pairs = [block for both in zip(mains, strips) for block in both]

    def total(pieces):
        got = summed([pieces[0]] + [hop(piece, 1, turn) for piece, turn in zip(pieces[1:], TURNS)])
        return got, hop(got, 2, 1)

    def spread(chunk):
        return [chunk] + [hop(chunk, 1, turn) for turn in TURNS]

    sums = total(tally(at, pairs[4:], tally(at, pairs[:4])))
    ratio, count = ratio_of(True, *sums, sensor)
    videos, products = first_denoise(at, pairs, spread(ratio))
    ratios = spread(ratio_of(False, *total(products), sensor, count))
    blocks = []
    for n, turn in enumerate(TURNS):
        blocks.append(hop(last_denoise(at, pairs[2 + 2 * n : 4 + 2 * n], videos[1 + n], ratios), 0, 4 - turn))
    own = last_denoise(at, pairs[:2], videos[0], ratios)
    return join(at, [own] + blocks)[None]


def solution(mesh):
    return jax.shard_map(
        per_device,
        mesh=mesh,
        in_specs=(P("row", "col"), P("frame", "row", "col"), P("frame", "row", "col")),
        out_specs=P("frame", "row", "col"),
        check_vma=False,
    )
```

```python
import functools

import jax
import jax.numpy as jnp
from jax import lax
from jax.experimental import pallas as pl
from jax.experimental.pallas import tpu as pltpu
from jax.sharding import PartitionSpec as P

PROJ = 2
TV_ITERS = 5

tv_weight = 0.1
step_size = 0.125

ROWS = 512
COLS = 1024
QUARTER = ROWS // 4
HR = 16
HC = 128
WINDOW = QUARTER + 2 * HR
TILES = COLS // HC + 1
MAIN = WINDOW - HR
KEPT = 12
STRIP = COLS // HC * KEPT
SIDE = 2 * HR
PACKED = COLS // HC * MAIN + STRIP + SIDE
CHUNK = PACKED // 4
PAD = 8
BLOCK = 40
TINY = 1e-35
TURNS = (1, 3, 2)

ROW, COL, START, STRIP_AT, OUTSIDE, SOURCE, TARGET, HALF, PLACE = 0, 1, 2, 6, 10, 14, 18, 22, 23


VMEM = pl.BlockSpec(memory_space=pltpu.VMEM)
HBM = pl.BlockSpec(memory_space=pltpu.HBM)
SMEM = pl.BlockSpec(memory_space=pltpu.SMEM)


TURNED = pltpu.VMEM((HC, 2 * HC), jnp.float32)


def near(*blocks):
    return [pltpu.with_memory_space_constraint(block, pltpu.VMEM) for block in blocks]


def grant(mib):
    return pltpu.CompilerParams(vmem_limit_bytes=mib << 20)


def f32(*shape):
    return jax.ShapeDtypeStruct(shape, jnp.float32)


def shifted(level, distance):
    pairs = []
    for frame in range(32):
        z, x, y = frame // 8, (frame // 2) % 4, frame % 2
        for core in range(2):
            tz, tx, ty = z, x, y
            if level == 2:
                ty = (y + distance) % 2
            elif (level == 0) == (core == 0):
                tz = (z + distance) % 4
            else:
                tx = (x + distance) % 4
            pairs.append((frame * 2 + core, (tz * 8 + tx * 2 + ty) * 2 + core))
    return pairs


def hop(block, level, distance):
    return lax.ppermute(block, ("frame", "col"), shifted(level, distance))


def window_start(quarter, row):
    return jnp.clip(quarter * QUARTER - HR * (1 - row), 0, ROWS - MAIN)


def cut_kernel(at_ref, masks_ref, video_ref, sensor_ref, *refs):
    mains, strips_ref, main_ref, edge_ref, end_ref, corner_ref, sems = refs[:4], *refs[4:]
    copies = []

    def copy(source, target):
        copies.append(pltpu.make_async_copy(source, target, sems.at[len(copies)]))
        copies[-1].start()

    for k in (1, 2, 3, 0):
        rows = pl.ds(pl.multiple_of(at_ref[START + k], HR), MAIN)
        copy(masks_ref.at[rows, :], mains[k].at[0])
        copy(video_ref.at[rows, :], mains[k].at[1])
    rows = pl.ds(pl.multiple_of((1 - at_ref[ROW]) * (ROWS - HR), HR), HR)
    cols = pl.ds(pl.multiple_of((1 - at_ref[COL]) * (COLS - HC), HC), HC)
    for n, source in enumerate((masks_ref, video_ref, sensor_ref)):
        copy(source.at[:, cols], edge_ref.at[n])
        copy(source.at[rows, :], end_ref.at[n])
        copy(source.at[rows, cols], corner_ref.at[n])
        for k in range(4 if n < 2 else 1):
            copy(source.at[pl.ds(pl.multiple_of(at_ref[STRIP_AT + k], HR), HR), :], strips_ref.at[4 * n + k])
    copy(sensor_ref.at[pl.ds(pl.multiple_of(at_ref[START], HR), MAIN), :], main_ref)
    for one in copies:
        one.wait()


def cut(at, masks, video, sensor):
    return pl.pallas_call(
        cut_kernel,
        out_shape=(f32(2, MAIN, COLS),) * 4 + (f32(9, HR, COLS), f32(MAIN, COLS), f32(3, ROWS, HC), f32(3, HR, COLS), f32(3, HR, HC)),
        in_specs=[SMEM] + [HBM] * 3,
        out_specs=(VMEM,) * 9,
        scratch_shapes=[pltpu.SemaphoreType.DMA((27,))],
        name="cut",
        compiler_params=grant(24),
    )(at, *[pltpu.with_memory_space_constraint(a, pltpu.HBM) for a in (masks, video, sensor)])


def kept_rows(strip, row):
    return jnp.where(row == 0, strip[:KEPT], strip[HR - KEPT :])


def strip_rows(kept, row):
    outer = jnp.zeros((HR - KEPT, kept.shape[1]), kept.dtype)
    return jnp.where(row == 0, jnp.concatenate([kept, outer], 0), jnp.concatenate([outer, kept], 0))


def side_rows(col):
    return pl.ds(pl.multiple_of(col * (HC - HR), HR), HR)


def turn_side(rows, turned_ref, col):
    turned_ref[:, :HC] = rows[:HC].T
    turned_ref[:, HC:] = rows[HC:].T
    side = side_rows(col)
    return turned_ref[side, :HC], turned_ref[side, HC:]


def halo_tile(side, turned_ref, col):
    turned_ref[side_rows(col), :HC] = side[:HR]
    turned_ref[side_rows(col), HC:] = side[HR:]
    return turned_ref[:, :HC].T, turned_ref[:, HC:].T[: WINDOW - HC]


def strips_kernel(at_ref, strips_ref, main_ref, beside_ref, below_ref, corner_ref, *refs):
    outs, sensor_ref, cols_ref, packed_ref, turned_ref = refs[:4], *refs[4:]
    row = at_ref[ROW]
    own = pl.multiple_of(row * HR, HR)
    other = pl.multiple_of((1 - row) * ROWS, HR)
    cols_ref[ROWS + HR :, :] = jnp.zeros((2 * HC - WINDOW, HC), jnp.float32)
    for n in range(3):
        cols_ref[pl.ds(own, ROWS), :] = beside_ref[n]
        cols_ref[pl.ds(other, HR), :] = corner_ref[n]
        for k in range(4 if n < 2 else 1):
            start = pl.multiple_of(at_ref[START + k], HR)
            strip = kept_rows(jnp.where(at_ref[OUTSIDE + k] == 1, below_ref[n], strips_ref[4 * n + k]), row)
            upper, lower = turn_side(cols_ref[pl.ds(start, 2 * HC), :], turned_ref, at_ref[COL])
            target, base = (outs[k].at[n], 0) if n < 2 else (packed_ref, MAIN * (TILES - 1))
            for t in range(TILES - 1):
                if n == 2:
                    target[t * MAIN : (t + 1) * MAIN, :] = main_ref[:, t * HC : (t + 1) * HC]
                target[base + t * KEPT : base + (t + 1) * KEPT, :] = strip[:, t * HC : (t + 1) * HC]
            target[base + STRIP : base + STRIP + HR, :] = upper
            target[base + STRIP + HR : base + STRIP + SIDE, :] = lower
    sensor_ref[...] = packed_ref[pl.ds(pl.multiple_of(at_ref[TARGET], PAD), CHUNK), :]


def cut_strips(at, *blocks):
    return pl.pallas_call(
        strips_kernel,
        out_shape=(f32(2, STRIP + SIDE, HC),) * 4 + (f32(CHUNK, HC),),
        in_specs=[SMEM] + [VMEM] * 5,
        out_specs=(VMEM,) * 5,
        scratch_shapes=[pltpu.VMEM((ROWS + HR + 2 * HC - WINDOW, HC), jnp.float32), pltpu.VMEM((PACKED, HC), jnp.float32), TURNED],
        name="strips",
        compiler_params=grant(20),
    )(at, *near(*blocks))


def sum_kernel(*refs):
    refs[-1][...] = (refs[0][...] + refs[1][...]) + (refs[2][...] + refs[3][...])


def summed(blocks):
    return pl.pallas_call(
        sum_kernel,
        out_shape=f32(*blocks[0].shape),
        in_specs=[VMEM] * 4,
        out_specs=VMEM,
        name="summed",
        compiler_params=grant(8),
    )(*near(*blocks))


def first_ratio_kernel(mine_ref, other_ref, sensor_ref, ratio_ref, count_ref):
    count = mine_ref[0] + other_ref[0]
    count_ref[...] = count
    ratio_ref[...] = (sensor_ref[...] - (mine_ref[1] + other_ref[1])) / count


def ratio_kernel(mine_ref, other_ref, sensor_ref, count_ref, ratio_ref):
    ratio_ref[...] = (sensor_ref[...] - (mine_ref[...] + other_ref[...])) / count_ref[...]


def ratio_of(first, *blocks):
    chunk = f32(CHUNK, HC)
    return pl.pallas_call(
        first_ratio_kernel if first else ratio_kernel,
        out_shape=(chunk, chunk) if first else chunk,
        in_specs=[VMEM] * len(blocks),
        out_specs=(VMEM, VMEM) if first else VMEM,
        name="first_ratio" if first else "ratio",
        compiler_params=grant(8),
    )(*near(*blocks))


def packed_parts():
    base = MAIN * (TILES - 1)
    for t in range(TILES - 1):
        yield t, slice(t * MAIN, (t + 1) * MAIN), 0, (slice(0, MAIN), slice(t * HC, (t + 1) * HC))
    for t in range(TILES - 1):
        yield t, slice(base + t * KEPT, base + (t + 1) * KEPT), 1, (slice(t * KEPT, (t + 1) * KEPT), slice(None))
    yield None, slice(base + STRIP, PACKED), 1, (slice(STRIP, STRIP + SIDE), slice(None))


def tiled_place(t, source, row, col):
    if source == 0:
        return col + t, pl.ds(pl.multiple_of(row * HR, HR), MAIN)
    return col + t, pl.ds(pl.multiple_of((1 - row) * MAIN, HR), HR)


def write_pieces(at_ref, whole_ref, outs):
    for k, out in enumerate(outs):
        piece = (pl.ds(pl.multiple_of(at_ref[TARGET + k], PAD), CHUNK), slice(None))
        for n in range(2) if len(out.shape) == 3 else (None,):
            lead = () if n is None else (n,)
            out[lead + (slice(None), slice(None))] = whole_ref[lead + piece]


def tally_kernel(at_ref, *refs, last):
    before = refs[0] if last else None
    frames = refs[1:5] if last else refs[:4]
    outs = refs[5:9] if last else refs[4:]
    sums_ref = refs[9] if last else refs[4]
    for _, packed, source, cut in packed_parts():
        count = before[0, packed, :] if last else 0.0
        measured = before[1, packed, :] if last else 0.0
        for k in range(2):
            pair = frames[2 * k + source]
            masks = pair[(0,) + cut]
            count += masks * masks
            measured += masks * pair[(1,) + cut]
        sums_ref[0, packed, :] = count
        sums_ref[1, packed, :] = measured
    if last:
        write_pieces(at_ref, sums_ref, outs)


def tally(at, frames, before=None):
    last = before is not None
    return pl.pallas_call(
        functools.partial(tally_kernel, last=last),
        out_shape=(f32(2, CHUNK, HC),) * 4 if last else f32(2, PACKED, HC),
        in_specs=[SMEM] + [VMEM] * (5 if last else 4),
        out_specs=(VMEM,) * 4 if last else VMEM,
        scratch_shapes=[pltpu.VMEM((2, PACKED, HC), jnp.float32)] if last else [],
        name="tally_last" if last else "tally",
        compiler_params=grant(20),
    )(at, *near(*([before] if last else []), *frames))


def tv_steps(f_ref, pr_ref, pc_ref, w_ref, frame, at, rows):
    tiles, _, lanes = f_ref.shape[1:]
    lane = lax.broadcasted_iota(jnp.int32, (rows, lanes), 1)

    def dual():
        before = 0.0
        for t in range(tiles):
            pc = pc_ref[t, :rows, :]
            turned = pltpu.roll(pc, 1, 1)
            left = jnp.where(lane == 0, before, turned)
            before = turned
            pr = pr_ref[t, PAD : PAD + rows, :]
            up = pr_ref[t, PAD - 1 : PAD - 1 + rows, :]
            w_ref[t, :rows, :] = step_size * ((pr - up) + (pc - left)) - f_ref[frame, t, pl.ds(at, rows), :]
        w_ref[:, rows : rows + 1, :] = w_ref[:, rows - 1 : rows, :]

    def update(start):
        for r in range(0, rows, BLOCK):
            n = min(BLOCK, rows - r)
            turned = pltpu.roll(w_ref[0, r : r + n, :], lanes - 1, 1)
            for t in range(tiles):
                w = w_ref[t, r : r + n, :]
                following = pltpu.roll(w_ref[t + 1, r : r + n, :], lanes - 1, 1) if t + 1 < tiles else w
                right = jnp.where(lane[:n] == lanes - 1, following, turned)
                turned = following
                gr = w_ref[t, r + 1 : r + n + 1, :] - w
                gc = right - w
                s = gr * gr + gc * gc
                inv = 1.0 / (1.0 + s * lax.rsqrt(jnp.maximum(s, TINY)))
                if not start:
                    gr = pr_ref[t, PAD + r : PAD + r + n, :] + gr
                    gc = pc_ref[t, r : r + n, :] + gc
                pr_ref[t, PAD + r : PAD + r + n, :] = gr * inv
                pc_ref[t, r : r + n, :] = gc * inv

    for t in range(tiles):
        w_ref[t, :rows, :] = -f_ref[frame, t, pl.ds(at, rows), :]
    w_ref[:, rows : rows + 1, :] = w_ref[:, rows - 1 : rows, :]
    update(True)

    def iteration(_, carry):
        dual()
        update(False)
        return carry

    lax.fori_loop(1, TV_ITERS, iteration, 0)
    dual()


def load_ratio(at_ref, ratios, ratio_ref):
    for k, ratio in enumerate(ratios):
        ratio_ref[pl.ds(pl.multiple_of(at_ref[SOURCE + k], PAD), CHUNK), :] = ratio[...]


def first_kernel(at_ref, *refs):
    pairs, ratios, videos, products = refs[:8], refs[8:12], refs[12:16], refs[16:20]
    ratio_ref, f_ref, pr_ref, pc_ref, w_ref, turned_ref, product_ref, rows_ref = refs[20:]
    row = at_ref[ROW]
    col = at_ref[COL]
    halo = (1 - col) * (TILES - 1)
    load_ratio(at_ref, ratios, ratio_ref)
    turned_ref[...] = jnp.zeros((HC, 2 * HC), jnp.float32)
    scale = step_size / tv_weight
    pr_ref[:, :PAD, :] = jnp.zeros((TILES, PAD, HC), jnp.float32)
    for k in range(4):
        for t, packed, source, cut in packed_parts():
            pair = pairs[2 * k + source]
            noisy = scale * (pair[(1,) + cut] + pair[(0,) + cut] * ratio_ref[packed, :])
            if t is None:
                f_ref[k, halo, :HC, :], f_ref[k, halo, HC:, :] = halo_tile(noisy, turned_ref, col)
            else:
                tile, rows = tiled_place(t, source, row, col)
                f_ref[k, tile, rows, :] = strip_rows(noisy, row) if source else noisy

    def one(k, carry):
        tv_steps(f_ref, pr_ref, pc_ref, w_ref, k, 0, WINDOW)
        for t in range(TILES):
            f_ref[k, t] = (-tv_weight / step_size) * w_ref[t, :WINDOW, :]
        return carry

    lax.fori_loop(0, 4, one, 0)
    rows_ref[WINDOW:, :] = jnp.zeros((2 * HC - WINDOW, HC), jnp.float32)
    for t, packed, source, cut in packed_parts():
        product = 0.0
        for k in range(4):
            if t is None:
                rows_ref[:WINDOW, :] = f_ref[k, halo]
                video = jnp.concatenate(turn_side(rows_ref[...], turned_ref, col), 0)
            else:
                tile, rows = tiled_place(t, source, row, col)
                video = f_ref[k, tile, rows, :]
                video = kept_rows(video, row) if source else video
            product += video * pairs[2 * k + source][(0,) + cut]
        product_ref[packed, :] = product
    for k in range(4):
        videos[k][...] = f_ref[k]
    write_pieces(at_ref, product_ref, products)


def tv_scratch(frames):
    return [
        pltpu.VMEM((PACKED, HC), jnp.float32),
        pltpu.VMEM((frames, TILES, WINDOW, HC), jnp.float32),
        pltpu.VMEM((TILES, WINDOW + 8, HC), jnp.float32),
        pltpu.VMEM((TILES, WINDOW + 16, HC), jnp.float32),
        pltpu.VMEM((TILES, WINDOW + 24, HC), jnp.float32),
        TURNED,
    ]


def first_denoise(at, pairs, ratios):
    out = pl.pallas_call(
        first_kernel,
        out_shape=(f32(TILES, WINDOW, HC),) * 4 + (f32(CHUNK, HC),) * 4,
        in_specs=[SMEM] + [VMEM] * 12,
        out_specs=(VMEM,) * 8,
        scratch_shapes=tv_scratch(4) + [pltpu.VMEM((PACKED, HC), jnp.float32), pltpu.VMEM((2 * HC, HC), jnp.float32)],
        name="tv_first",
        compiler_params=grant(36),
    )(at, *near(*pairs, *ratios))
    return out[:4], out[4:]


def last_kernel(at_ref, main_ref, strip_ref, video_ref, *refs):
    ratios, out_ref = refs[:4], refs[4]
    ratio_ref, f_ref, pr_ref, pc_ref, w_ref, turned_ref = refs[5:]
    row = at_ref[ROW]
    col = at_ref[COL]
    halo = (1 - col) * (TILES - 1)
    load_ratio(at_ref, ratios, ratio_ref)
    turned_ref[...] = jnp.zeros((HC, 2 * HC), jnp.float32)
    scale = step_size / tv_weight
    pr_ref[:, :PAD, :] = jnp.zeros((TILES, PAD, HC), jnp.float32)
    pair = (main_ref, strip_ref)
    for t, packed, source, cut in packed_parts():
        change = pair[source][(0,) + cut] * ratio_ref[packed, :]
        if t is None:
            upper, lower = halo_tile(change, turned_ref, col)
            f_ref[0, halo, :HC, :] = scale * (video_ref[halo, :HC, :] + upper)
            f_ref[0, halo, HC:, :] = scale * (video_ref[halo, HC:, :] + lower)
        else:
            tile, rows = tiled_place(t, source, row, col)
            change = strip_rows(change, row) if source else change
            f_ref[0, tile, rows, :] = scale * (video_ref[tile, rows, :] + change)
    half = pl.multiple_of(at_ref[HALF], PAD)
    tv_steps(f_ref, pr_ref, pc_ref, w_ref, 0, half, MAIN)
    for t in range(TILES - 1):
        out_ref[:, t * HC : (t + 1) * HC] = (-tv_weight / step_size) * w_ref[col + t, pl.ds(half, QUARTER), :]


def last_denoise(at, pair, video, ratios):
    return pl.pallas_call(
        last_kernel,
        out_shape=f32(QUARTER, COLS),
        in_specs=[SMEM] + [VMEM] * 7,
        out_specs=VMEM,
        scratch_shapes=tv_scratch(1),
        name="tv_last",
        compiler_params=grant(16),
    )(at, *near(*pair, video, *ratios))


def join_kernel(at_ref, *refs):
    blocks, out_ref, sems = refs[:4], refs[4], refs[5]
    copies = []
    for k, block in enumerate(blocks):
        place = out_ref.at[pl.ds(pl.multiple_of(at_ref[PLACE + k], QUARTER), QUARTER), :]
        copies.append(pltpu.make_async_copy(block, place, sems.at[k]))
        copies[-1].start()
    for one in copies:
        one.wait()


def join(at, blocks):
    return pl.pallas_call(
        join_kernel,
        out_shape=f32(ROWS, COLS),
        in_specs=[SMEM] + [VMEM] * 4,
        out_specs=HBM,
        scratch_shapes=[pltpu.SemaphoreType.DMA((4,))],
        name="join",
        compiler_params=grant(8),
    )(at, *near(*blocks))


def table(*values):
    return jnp.stack([jnp.asarray(value, jnp.int32) for value in values])


def per_device(measurement, masks, estimate):
    masks = masks[0]
    video = estimate[0]
    row = lax.axis_index("row")
    col = lax.axis_index("col")
    frame = lax.axis_index("frame")
    z, x = frame // 8, (frame // 2) % 4
    mine = jnp.where(col == 0, z, x)
    other = jnp.where(col == 0, x, z)

    starts = [window_start((mine + turn) % 4, row) for turn in (0,) + TURNS]
    strip_at = [jnp.where(row == 0, jnp.minimum(start + MAIN, ROWS - HR), jnp.maximum(start - HR, 0)) for start in starts]
    outside = [start == (ROWS - MAIN) * (1 - row) for start in starts]
    sources = [(other - turn) % 4 * CHUNK for turn in (0,) + TURNS]
    targets = [(other + turn) % 4 * CHUNK for turn in (0,) + TURNS]
    half = (mine * QUARTER - HR * (1 - row) - starts[0] + HR) // 2
    places = [(mine + turn) % 4 * QUARTER for turn in (0,) + TURNS]
    at = table(row, col, *starts, *strip_at, *outside, *sources, *targets, half, *places)

    *mains, strips, sensor, edge, end, corner = cut(at, masks, video, measurement)
    mains = [mains[0]] + [hop(mains[1 + n], 0, turn) for n, turn in enumerate(TURNS)]
    swap = [(0, 1), (1, 0)]
    beside = lax.ppermute(edge, "col", swap)
    below = lax.ppermute(end, "row", swap)
    corner = lax.ppermute(corner, ("row", "col"), [(0, 3), (3, 0), (1, 2), (2, 1)])
    *strips, sensor = cut_strips(at, strips, sensor, beside, below, corner)
    strips = [strips[0]] + [hop(strips[1 + n], 0, turn) for n, turn in enumerate(TURNS)]
    pairs = [block for both in zip(mains, strips) for block in both]

    def total(pieces):
        got = summed([pieces[0]] + [hop(piece, 1, turn) for piece, turn in zip(pieces[1:], TURNS)])
        return got, hop(got, 2, 1)

    def spread(chunk):
        return [chunk] + [hop(chunk, 1, turn) for turn in TURNS]

    sums = total(tally(at, pairs[4:], tally(at, pairs[:4])))
    ratio, count = ratio_of(True, *sums, sensor)
    videos, products = first_denoise(at, pairs, spread(ratio))
    ratios = spread(ratio_of(False, *total(products), sensor, count))
    blocks = []
    for n, turn in enumerate(TURNS):
        blocks.append(hop(last_denoise(at, pairs[2 + 2 * n : 4 + 2 * n], videos[1 + n], ratios), 0, 4 - turn))
    own = last_denoise(at, pairs[:2], videos[0], ratios)
    return join(at, [own] + blocks)[None]


def solution(mesh):
    return jax.shard_map(
        per_device,
        mesh=mesh,
        in_specs=(P("row", "col"), P("frame", "row", "col"), P("frame", "row", "col")),
        out_specs=P("frame", "row", "col"),
        check_vma=False,
    )
```

```python
import functools

import jax
import jax.numpy as jnp
from jax import lax
from jax.experimental import pallas as pl
from jax.experimental.pallas import tpu as pltpu
from jax.sharding import PartitionSpec as P

PROJ = 2
TV_ITERS = 5

tv_weight = 0.1
step_size = 0.125

ROWS = 512
COLS = 1024
QUARTER = ROWS // 4
HR = 16
HC = 128
WINDOW = QUARTER + 2 * HR
TILES = COLS // HC + 1
MAIN = WINDOW - HR
KEPT = 12
STRIP = COLS // HC * KEPT
SIDE = 2 * HR
PACKED = COLS // HC * MAIN + STRIP + SIDE
CHUNK = PACKED // 4
PAD = 8
BLOCK = 40
TINY = 1e-35
TURNS = (1, 3, 2)

ROW, COL, START, STRIP_AT, OUTSIDE, SOURCE, TARGET, HALF, PLACE = 0, 1, 2, 6, 10, 14, 18, 22, 23


VMEM = pl.BlockSpec(memory_space=pltpu.VMEM)
HBM = pl.BlockSpec(memory_space=pltpu.HBM)
SMEM = pl.BlockSpec(memory_space=pltpu.SMEM)


TURNED = pltpu.VMEM((HC, 2 * HC), jnp.float32)


def near(*blocks):
    return [pltpu.with_memory_space_constraint(block, pltpu.VMEM) for block in blocks]


def grant(mib):
    return pltpu.CompilerParams(vmem_limit_bytes=mib << 20)


def f32(*shape):
    return jax.ShapeDtypeStruct(shape, jnp.float32)


def shifted(level, distance):
    pairs = []
    for frame in range(32):
        z, x, y = frame // 8, (frame // 2) % 4, frame % 2
        for core in range(2):
            tz, tx, ty = z, x, y
            if level == 2:
                ty = (y + distance) % 2
            elif (level == 0) == (core == 0):
                tz = (z + distance) % 4
            else:
                tx = (x + distance) % 4
            pairs.append((frame * 2 + core, (tz * 8 + tx * 2 + ty) * 2 + core))
    return pairs


def hop(block, level, distance):
    return lax.ppermute(block, ("frame", "col"), shifted(level, distance))


def window_start(quarter, row):
    return jnp.clip(quarter * QUARTER - HR * (1 - row), 0, ROWS - MAIN)


def cut_kernel(at_ref, masks_ref, video_ref, sensor_ref, *refs):
    mains, strips_ref, main_ref, edge_ref, end_ref, corner_ref, sems = refs[:4], *refs[4:]
    copies = []

    def copy(source, target):
        copies.append(pltpu.make_async_copy(source, target, sems.at[len(copies)]))
        copies[-1].start()

    for k in (1, 2, 3, 0):
        rows = pl.ds(pl.multiple_of(at_ref[START + k], HR), MAIN)
        copy(masks_ref.at[rows, :], mains[k].at[0])
        copy(video_ref.at[rows, :], mains[k].at[1])
    rows = pl.ds(pl.multiple_of((1 - at_ref[ROW]) * (ROWS - HR), HR), HR)
    cols = pl.ds(pl.multiple_of((1 - at_ref[COL]) * (COLS - HC), HC), HC)
    for n, source in enumerate((masks_ref, video_ref, sensor_ref)):
        copy(source.at[:, cols], edge_ref.at[n])
        copy(source.at[rows, :], end_ref.at[n])
        copy(source.at[rows, cols], corner_ref.at[n])
        for k in range(4 if n < 2 else 1):
            copy(source.at[pl.ds(pl.multiple_of(at_ref[STRIP_AT + k], HR), HR), :], strips_ref.at[4 * n + k])
    copy(sensor_ref.at[pl.ds(pl.multiple_of(at_ref[START], HR), MAIN), :], main_ref)
    for one in copies:
        one.wait()


def cut(at, masks, video, sensor):
    return pl.pallas_call(
        cut_kernel,
        out_shape=(f32(2, MAIN, COLS),) * 4 + (f32(9, HR, COLS), f32(MAIN, COLS), f32(3, ROWS, HC), f32(3, HR, COLS), f32(3, HR, HC)),
        in_specs=[SMEM] + [HBM] * 3,
        out_specs=(VMEM,) * 9,
        scratch_shapes=[pltpu.SemaphoreType.DMA((27,))],
        name="cut",
        compiler_params=grant(24),
    )(at, *[pltpu.with_memory_space_constraint(a, pltpu.HBM) for a in (masks, video, sensor)])


def kept_rows(strip, row):
    return jnp.where(row == 0, strip[:KEPT], strip[HR - KEPT :])


def strip_rows(kept, row):
    outer = jnp.zeros((HR - KEPT, kept.shape[1]), kept.dtype)
    return jnp.where(row == 0, jnp.concatenate([kept, outer], 0), jnp.concatenate([outer, kept], 0))


def side_rows(col):
    return pl.ds(pl.multiple_of(col * (HC - HR), HR), HR)


def turn_side(rows, turned_ref, col):
    turned_ref[:, :HC] = rows[:HC].T
    turned_ref[:, HC:] = rows[HC:].T
    side = side_rows(col)
    return turned_ref[side, :HC], turned_ref[side, HC:]


def halo_tile(side, turned_ref, col):
    turned_ref[side_rows(col), :HC] = side[:HR]
    turned_ref[side_rows(col), HC:] = side[HR:]
    return turned_ref[:, :HC].T, turned_ref[:, HC:].T[: WINDOW - HC]


def strips_kernel(at_ref, strips_ref, main_ref, beside_ref, below_ref, corner_ref, *refs):
    outs, sensor_ref, cols_ref, packed_ref, turned_ref = refs[:4], *refs[4:]
    row = at_ref[ROW]
    own = pl.multiple_of(row * HR, HR)
    other = pl.multiple_of((1 - row) * ROWS, HR)
    cols_ref[ROWS + HR :, :] = jnp.zeros((2 * HC - WINDOW, HC), jnp.float32)
    for n in range(3):
        cols_ref[pl.ds(own, ROWS), :] = beside_ref[n]
        cols_ref[pl.ds(other, HR), :] = corner_ref[n]
        for k in range(4 if n < 2 else 1):
            start = pl.multiple_of(at_ref[START + k], HR)
            strip = kept_rows(jnp.where(at_ref[OUTSIDE + k] == 1, below_ref[n], strips_ref[4 * n + k]), row)
            upper, lower = turn_side(cols_ref[pl.ds(start, 2 * HC), :], turned_ref, at_ref[COL])
            target, base = (outs[k].at[n], 0) if n < 2 else (packed_ref, MAIN * (TILES - 1))
            for t in range(TILES - 1):
                if n == 2:
                    target[t * MAIN : (t + 1) * MAIN, :] = main_ref[:, t * HC : (t + 1) * HC]
                target[base + t * KEPT : base + (t + 1) * KEPT, :] = strip[:, t * HC : (t + 1) * HC]
            target[base + STRIP : base + STRIP + HR, :] = upper
            target[base + STRIP + HR : base + STRIP + SIDE, :] = lower
    sensor_ref[...] = packed_ref[pl.ds(pl.multiple_of(at_ref[TARGET], PAD), CHUNK), :]


def cut_strips(at, *blocks):
    return pl.pallas_call(
        strips_kernel,
        out_shape=(f32(2, STRIP + SIDE, HC),) * 4 + (f32(CHUNK, HC),),
        in_specs=[SMEM] + [VMEM] * 5,
        out_specs=(VMEM,) * 5,
        scratch_shapes=[pltpu.VMEM((ROWS + HR + 2 * HC - WINDOW, HC), jnp.float32), pltpu.VMEM((PACKED, HC), jnp.float32), TURNED],
        name="strips",
        compiler_params=grant(20),
    )(at, *near(*blocks))


def sum_kernel(*refs):
    refs[-1][...] = (refs[0][...] + refs[1][...]) + (refs[2][...] + refs[3][...])


def summed(blocks):
    return pl.pallas_call(
        sum_kernel,
        out_shape=f32(*blocks[0].shape),
        in_specs=[VMEM] * 4,
        out_specs=VMEM,
        name="summed",
        compiler_params=grant(8),
    )(*near(*blocks))


def first_ratio_kernel(mine_ref, other_ref, sensor_ref, ratio_ref, count_ref):
    count = mine_ref[0] + other_ref[0]
    count_ref[...] = count
    ratio_ref[...] = (sensor_ref[...] - (mine_ref[1] + other_ref[1])) / count


def ratio_kernel(mine_ref, other_ref, sensor_ref, count_ref, ratio_ref):
    ratio_ref[...] = (sensor_ref[...] - (mine_ref[...] + other_ref[...])) / count_ref[...]


def ratio_of(first, *blocks):
    chunk = f32(CHUNK, HC)
    return pl.pallas_call(
        first_ratio_kernel if first else ratio_kernel,
        out_shape=(chunk, chunk) if first else chunk,
        in_specs=[VMEM] * len(blocks),
        out_specs=(VMEM, VMEM) if first else VMEM,
        name="first_ratio" if first else "ratio",
        compiler_params=grant(8),
    )(*near(*blocks))


def packed_parts():
    base = MAIN * (TILES - 1)
    for t in range(TILES - 1):
        yield t, slice(t * MAIN, (t + 1) * MAIN), 0, (slice(0, MAIN), slice(t * HC, (t + 1) * HC))
    for t in range(TILES - 1):
        yield t, slice(base + t * KEPT, base + (t + 1) * KEPT), 1, (slice(t * KEPT, (t + 1) * KEPT), slice(None))
    yield None, slice(base + STRIP, PACKED), 1, (slice(STRIP, STRIP + SIDE), slice(None))


def tiled_place(t, source, row, col):
    if source == 0:
        return col + t, pl.ds(pl.multiple_of(row * HR, HR), MAIN)
    return col + t, pl.ds(pl.multiple_of((1 - row) * MAIN, HR), HR)


def write_pieces(at_ref, whole_ref, outs):
    for k, out in enumerate(outs):
        piece = (pl.ds(pl.multiple_of(at_ref[TARGET + k], PAD), CHUNK), slice(None))
        for n in range(2) if len(out.shape) == 3 else (None,):
            lead = () if n is None else (n,)
            out[lead + (slice(None), slice(None))] = whole_ref[lead + piece]


def tally_kernel(at_ref, *refs):
    pairs, outs, sums_ref = refs[:8], refs[8:12], refs[12]
    for _, packed, source, cut in packed_parts():
        count = 0.0
        measured = 0.0
        for k in range(4):
            masks = pairs[2 * k + source][(0,) + cut]
            count += masks * masks
            measured += masks * pairs[2 * k + source][(1,) + cut]
        sums_ref[0, packed, :] = count
        sums_ref[1, packed, :] = measured
    write_pieces(at_ref, sums_ref, outs)


def tally(at, pairs):
    return pl.pallas_call(
        tally_kernel,
        out_shape=(f32(2, CHUNK, HC),) * 4,
        in_specs=[SMEM] + [VMEM] * 8,
        out_specs=(VMEM,) * 4,
        scratch_shapes=[pltpu.VMEM((2, PACKED, HC), jnp.float32)],
        name="tally",
        compiler_params=grant(20),
    )(at, *near(*pairs))


def tv_steps(f_ref, pr_ref, pc_ref, w_ref, frame, at, rows):
    tiles, _, lanes = f_ref.shape[1:]
    lane = lax.broadcasted_iota(jnp.int32, (rows, lanes), 1)

    def dual():
        before = 0.0
        for t in range(tiles):
            pc = pc_ref[t, :rows, :]
            turned = pltpu.roll(pc, 1, 1)
            left = jnp.where(lane == 0, before, turned)
            before = turned
            pr = pr_ref[t, PAD : PAD + rows, :]
            up = pr_ref[t, PAD - 1 : PAD - 1 + rows, :]
            w_ref[t, :rows, :] = step_size * ((pr - up) + (pc - left)) - f_ref[frame, t, pl.ds(at, rows), :]
        w_ref[:, rows : rows + 1, :] = w_ref[:, rows - 1 : rows, :]

    def update(start):
        for r in range(0, rows, BLOCK):
            n = min(BLOCK, rows - r)
            turned = pltpu.roll(w_ref[0, r : r + n, :], lanes - 1, 1)
            for t in range(tiles):
                w = w_ref[t, r : r + n, :]
                following = pltpu.roll(w_ref[t + 1, r : r + n, :], lanes - 1, 1) if t + 1 < tiles else w
                right = jnp.where(lane[:n] == lanes - 1, following, turned)
                turned = following
                gr = w_ref[t, r + 1 : r + n + 1, :] - w
                gc = right - w
                s = gr * gr + gc * gc
                inv = 1.0 / (1.0 + s * lax.rsqrt(jnp.maximum(s, TINY)))
                if not start:
                    gr = pr_ref[t, PAD + r : PAD + r + n, :] + gr
                    gc = pc_ref[t, r : r + n, :] + gc
                pr_ref[t, PAD + r : PAD + r + n, :] = gr * inv
                pc_ref[t, r : r + n, :] = gc * inv

    for t in range(tiles):
        w_ref[t, :rows, :] = -f_ref[frame, t, pl.ds(at, rows), :]
    w_ref[:, rows : rows + 1, :] = w_ref[:, rows - 1 : rows, :]
    update(True)

    def iteration(_, carry):
        dual()
        update(False)
        return carry

    lax.fori_loop(1, TV_ITERS, iteration, 0)
    dual()


def load_ratio(at_ref, ratios, ratio_ref):
    for k, ratio in enumerate(ratios):
        ratio_ref[pl.ds(pl.multiple_of(at_ref[SOURCE + k], PAD), CHUNK), :] = ratio[...]


def first_kernel(at_ref, *refs):
    pairs, ratios, videos, products = refs[:8], refs[8:12], refs[12:16], refs[16:20]
    ratio_ref, f_ref, pr_ref, pc_ref, w_ref, turned_ref, product_ref, rows_ref = refs[20:]
    row = at_ref[ROW]
    col = at_ref[COL]
    halo = (1 - col) * (TILES - 1)
    load_ratio(at_ref, ratios, ratio_ref)
    turned_ref[...] = jnp.zeros((HC, 2 * HC), jnp.float32)
    scale = step_size / tv_weight
    pr_ref[:, :PAD, :] = jnp.zeros((TILES, PAD, HC), jnp.float32)
    for k in range(4):
        for t, packed, source, cut in packed_parts():
            pair = pairs[2 * k + source]
            noisy = scale * (pair[(1,) + cut] + pair[(0,) + cut] * ratio_ref[packed, :])
            if t is None:
                f_ref[k, halo, :HC, :], f_ref[k, halo, HC:, :] = halo_tile(noisy, turned_ref, col)
            else:
                tile, rows = tiled_place(t, source, row, col)
                f_ref[k, tile, rows, :] = strip_rows(noisy, row) if source else noisy

    def one(k, carry):
        tv_steps(f_ref, pr_ref, pc_ref, w_ref, k, 0, WINDOW)
        for t in range(TILES):
            f_ref[k, t] = (-tv_weight / step_size) * w_ref[t, :WINDOW, :]
        return carry

    lax.fori_loop(0, 4, one, 0)
    rows_ref[WINDOW:, :] = jnp.zeros((2 * HC - WINDOW, HC), jnp.float32)
    for t, packed, source, cut in packed_parts():
        product = 0.0
        for k in range(4):
            if t is None:
                rows_ref[:WINDOW, :] = f_ref[k, halo]
                video = jnp.concatenate(turn_side(rows_ref[...], turned_ref, col), 0)
            else:
                tile, rows = tiled_place(t, source, row, col)
                video = f_ref[k, tile, rows, :]
                video = kept_rows(video, row) if source else video
            product += video * pairs[2 * k + source][(0,) + cut]
        product_ref[packed, :] = product
    for k in range(4):
        videos[k][...] = f_ref[k]
    write_pieces(at_ref, product_ref, products)


def tv_scratch(frames):
    return [
        pltpu.VMEM((PACKED, HC), jnp.float32),
        pltpu.VMEM((frames, TILES, WINDOW, HC), jnp.float32),
        pltpu.VMEM((TILES, WINDOW + 8, HC), jnp.float32),
        pltpu.VMEM((TILES, WINDOW + 16, HC), jnp.float32),
        pltpu.VMEM((TILES, WINDOW + 24, HC), jnp.float32),
        TURNED,
    ]


def first_denoise(at, pairs, ratios):
    out = pl.pallas_call(
        first_kernel,
        out_shape=(f32(TILES, WINDOW, HC),) * 4 + (f32(CHUNK, HC),) * 4,
        in_specs=[SMEM] + [VMEM] * 12,
        out_specs=(VMEM,) * 8,
        scratch_shapes=tv_scratch(4) + [pltpu.VMEM((PACKED, HC), jnp.float32), pltpu.VMEM((2 * HC, HC), jnp.float32)],
        name="tv_first",
        compiler_params=grant(36),
    )(at, *near(*pairs, *ratios))
    return out[:4], out[4:]


def last_kernel(at_ref, main_ref, strip_ref, video_ref, *refs):
    ratios, out_ref = refs[:4], refs[4]
    ratio_ref, f_ref, pr_ref, pc_ref, w_ref, turned_ref = refs[5:]
    row = at_ref[ROW]
    col = at_ref[COL]
    halo = (1 - col) * (TILES - 1)
    load_ratio(at_ref, ratios, ratio_ref)
    turned_ref[...] = jnp.zeros((HC, 2 * HC), jnp.float32)
    scale = step_size / tv_weight
    pr_ref[:, :PAD, :] = jnp.zeros((TILES, PAD, HC), jnp.float32)
    pair = (main_ref, strip_ref)
    for t, packed, source, cut in packed_parts():
        change = pair[source][(0,) + cut] * ratio_ref[packed, :]
        if t is None:
            upper, lower = halo_tile(change, turned_ref, col)
            f_ref[0, halo, :HC, :] = scale * (video_ref[halo, :HC, :] + upper)
            f_ref[0, halo, HC:, :] = scale * (video_ref[halo, HC:, :] + lower)
        else:
            tile, rows = tiled_place(t, source, row, col)
            change = strip_rows(change, row) if source else change
            f_ref[0, tile, rows, :] = scale * (video_ref[tile, rows, :] + change)
    half = pl.multiple_of(at_ref[HALF], PAD)
    tv_steps(f_ref, pr_ref, pc_ref, w_ref, 0, half, MAIN)
    for t in range(TILES - 1):
        out_ref[:, t * HC : (t + 1) * HC] = (-tv_weight / step_size) * w_ref[col + t, pl.ds(half, QUARTER), :]


def last_denoise(at, pair, video, ratios):
    return pl.pallas_call(
        last_kernel,
        out_shape=f32(QUARTER, COLS),
        in_specs=[SMEM] + [VMEM] * 7,
        out_specs=VMEM,
        scratch_shapes=tv_scratch(1),
        name="tv_last",
        compiler_params=grant(16),
    )(at, *near(*pair, video, *ratios))


def join_kernel(at_ref, *refs):
    blocks, out_ref, sems = refs[:4], refs[4], refs[5]
    copies = []
    for k, block in enumerate(blocks):
        place = out_ref.at[pl.ds(pl.multiple_of(at_ref[PLACE + k], QUARTER), QUARTER), :]
        copies.append(pltpu.make_async_copy(block, place, sems.at[k]))
        copies[-1].start()
    for one in copies:
        one.wait()


def join(at, blocks):
    return pl.pallas_call(
        join_kernel,
        out_shape=f32(ROWS, COLS),
        in_specs=[SMEM] + [VMEM] * 4,
        out_specs=HBM,
        scratch_shapes=[pltpu.SemaphoreType.DMA((4,))],
        name="join",
        compiler_params=grant(8),
    )(at, *near(*blocks))


def table(*values):
    return jnp.stack([jnp.asarray(value, jnp.int32) for value in values])


def per_device(measurement, masks, estimate):
    masks = masks[0]
    video = estimate[0]
    row = lax.axis_index("row")
    col = lax.axis_index("col")
    frame = lax.axis_index("frame")
    z, x = frame // 8, (frame // 2) % 4
    mine = jnp.where(col == 0, z, x)
    other = jnp.where(col == 0, x, z)

    starts = [window_start((mine + turn) % 4, row) for turn in (0,) + TURNS]
    strip_at = [jnp.where(row == 0, jnp.minimum(start + MAIN, ROWS - HR), jnp.maximum(start - HR, 0)) for start in starts]
    outside = [start == (ROWS - MAIN) * (1 - row) for start in starts]
    sources = [(other - turn) % 4 * CHUNK for turn in (0,) + TURNS]
    targets = [(other + turn) % 4 * CHUNK for turn in (0,) + TURNS]
    half = (mine * QUARTER - HR * (1 - row) - starts[0] + HR) // 2
    places = [(mine + turn) % 4 * QUARTER for turn in (0,) + TURNS]
    at = table(row, col, *starts, *strip_at, *outside, *sources, *targets, half, *places)

    *mains, strips, sensor, edge, end, corner = cut(at, masks, video, measurement)
    mains = [mains[0]] + [hop(mains[1 + n], 0, turn) for n, turn in enumerate(TURNS)]
    swap = [(0, 1), (1, 0)]
    beside = lax.ppermute(edge, "col", swap)
    below = lax.ppermute(end, "row", swap)
    corner = lax.ppermute(corner, ("row", "col"), [(0, 3), (3, 0), (1, 2), (2, 1)])
    *strips, sensor = cut_strips(at, strips, sensor, beside, below, corner)
    strips = [strips[0]] + [hop(strips[1 + n], 0, turn) for n, turn in enumerate(TURNS)]
    pairs = [block for both in zip(mains, strips) for block in both]

    def total(pieces):
        got = summed([pieces[0]] + [hop(piece, 1, turn) for piece, turn in zip(pieces[1:], TURNS)])
        return got, hop(got, 2, 1)

    def spread(chunk):
        return [chunk] + [hop(chunk, 1, turn) for turn in TURNS]

    sums = total(tally(at, pairs))
    ratio, count = ratio_of(True, *sums, sensor)
    videos, products = first_denoise(at, pairs, spread(ratio))
    ratios = spread(ratio_of(False, *total(products), sensor, count))
    blocks = []
    for n, turn in enumerate(TURNS):
        blocks.append(hop(last_denoise(at, pairs[2 + 2 * n : 4 + 2 * n], videos[1 + n], ratios), 0, 4 - turn))
    own = last_denoise(at, pairs[:2], videos[0], ratios)
    return join(at, [own] + blocks)[None]


def solution(mesh):
    return jax.shard_map(
        per_device,
        mesh=mesh,
        in_specs=(P("row", "col"), P("frame", "row", "col"), P("frame", "row", "col")),
        out_specs=P("frame", "row", "col"),
        check_vma=False,
    )
```

```python
import functools

import jax
import jax.numpy as jnp
from jax import lax
from jax.experimental import pallas as pl
from jax.experimental.pallas import tpu as pltpu
from jax.sharding import PartitionSpec as P

PROJ = 2
TV_ITERS = 5

tv_weight = 0.1
step_size = 0.125

ROWS = 512
COLS = 1024
QUARTER = ROWS // 4
HR = 16
HC = 128
WINDOW = QUARTER + 2 * HR
TILES = COLS // HC + 1
MAIN = WINDOW - HR
KEPT = 12
STRIP = COLS // HC * KEPT
SIDE = 2 * HR
PACKED = COLS // HC * MAIN + STRIP + SIDE
CHUNK = PACKED // 4
PAD = 8
BLOCK = 32
TINY = 1e-35
TURNS = (1, 3, 2)

ROW, COL, START, STRIP_AT, OUTSIDE, SOURCE, TARGET, HALF, PLACE = 0, 1, 2, 6, 10, 14, 18, 22, 23


VMEM = pl.BlockSpec(memory_space=pltpu.VMEM)
HBM = pl.BlockSpec(memory_space=pltpu.HBM)
SMEM = pl.BlockSpec(memory_space=pltpu.SMEM)


TURNED = pltpu.VMEM((HC, 2 * HC), jnp.float32)


def near(*blocks):
    return [pltpu.with_memory_space_constraint(block, pltpu.VMEM) for block in blocks]


def grant(mib):
    return pltpu.CompilerParams(vmem_limit_bytes=mib << 20)


def f32(*shape):
    return jax.ShapeDtypeStruct(shape, jnp.float32)


def shifted(level, distance):
    pairs = []
    for frame in range(32):
        z, x, y = frame // 8, (frame // 2) % 4, frame % 2
        for core in range(2):
            tz, tx, ty = z, x, y
            if level == 2:
                ty = (y + distance) % 2
            elif (level == 0) == (core == 0):
                tz = (z + distance) % 4
            else:
                tx = (x + distance) % 4
            pairs.append((frame * 2 + core, (tz * 8 + tx * 2 + ty) * 2 + core))
    return pairs


def hop(block, level, distance):
    return lax.ppermute(block, ("frame", "col"), shifted(level, distance))


def window_start(quarter, row):
    return jnp.clip(quarter * QUARTER - HR * (1 - row), 0, ROWS - MAIN)


def cut_kernel(at_ref, masks_ref, video_ref, sensor_ref, *refs):
    mains, strips_ref, main_ref, edge_ref, end_ref, corner_ref, sems = refs[:4], *refs[4:]
    copies = []

    def copy(source, target):
        copies.append(pltpu.make_async_copy(source, target, sems.at[len(copies)]))
        copies[-1].start()

    for k in (1, 2, 3, 0):
        rows = pl.ds(pl.multiple_of(at_ref[START + k], HR), MAIN)
        copy(masks_ref.at[rows, :], mains[k].at[0])
        copy(video_ref.at[rows, :], mains[k].at[1])
    rows = pl.ds(pl.multiple_of((1 - at_ref[ROW]) * (ROWS - HR), HR), HR)
    cols = pl.ds(pl.multiple_of((1 - at_ref[COL]) * (COLS - HC), HC), HC)
    for n, source in enumerate((masks_ref, video_ref, sensor_ref)):
        copy(source.at[:, cols], edge_ref.at[n])
        copy(source.at[rows, :], end_ref.at[n])
        copy(source.at[rows, cols], corner_ref.at[n])
        for k in range(4 if n < 2 else 1):
            copy(source.at[pl.ds(pl.multiple_of(at_ref[STRIP_AT + k], HR), HR), :], strips_ref.at[4 * n + k])
    copy(sensor_ref.at[pl.ds(pl.multiple_of(at_ref[START], HR), MAIN), :], main_ref)
    for one in copies:
        one.wait()


def cut(at, masks, video, sensor):
    return pl.pallas_call(
        cut_kernel,
        out_shape=(f32(2, MAIN, COLS),) * 4 + (f32(9, HR, COLS), f32(MAIN, COLS), f32(3, ROWS, HC), f32(3, HR, COLS), f32(3, HR, HC)),
        in_specs=[SMEM] + [HBM] * 3,
        out_specs=(VMEM,) * 9,
        scratch_shapes=[pltpu.SemaphoreType.DMA((27,))],
        name="cut",
        compiler_params=grant(24),
    )(at, *[pltpu.with_memory_space_constraint(a, pltpu.HBM) for a in (masks, video, sensor)])


def kept_rows(strip, row):
    return jnp.where(row == 0, strip[:KEPT], strip[HR - KEPT :])


def strip_rows(kept, row):
    outer = jnp.zeros((HR - KEPT, kept.shape[1]), kept.dtype)
    return jnp.where(row == 0, jnp.concatenate([kept, outer], 0), jnp.concatenate([outer, kept], 0))


def side_rows(col):
    return pl.ds(pl.multiple_of(col * (HC - HR), HR), HR)


def turn_side(rows, turned_ref, col):
    turned_ref[:, :HC] = rows[:HC].T
    turned_ref[:, HC:] = rows[HC:].T
    side = side_rows(col)
    return turned_ref[side, :HC], turned_ref[side, HC:]


def halo_tile(side, turned_ref, col):
    turned_ref[side_rows(col), :HC] = side[:HR]
    turned_ref[side_rows(col), HC:] = side[HR:]
    return turned_ref[:, :HC].T, turned_ref[:, HC:].T[: WINDOW - HC]


def strips_kernel(at_ref, strips_ref, main_ref, beside_ref, below_ref, corner_ref, *refs):
    outs, sensor_ref, cols_ref, packed_ref, turned_ref = refs[:4], *refs[4:]
    row = at_ref[ROW]
    own = pl.multiple_of(row * HR, HR)
    other = pl.multiple_of((1 - row) * ROWS, HR)
    cols_ref[ROWS + HR :, :] = jnp.zeros((2 * HC - WINDOW, HC), jnp.float32)
    for n in range(3):
        cols_ref[pl.ds(own, ROWS), :] = beside_ref[n]
        cols_ref[pl.ds(other, HR), :] = corner_ref[n]
        for k in range(4 if n < 2 else 1):
            start = pl.multiple_of(at_ref[START + k], HR)
            strip = kept_rows(jnp.where(at_ref[OUTSIDE + k] == 1, below_ref[n], strips_ref[4 * n + k]), row)
            upper, lower = turn_side(cols_ref[pl.ds(start, 2 * HC), :], turned_ref, at_ref[COL])
            target, base = (outs[k].at[n], 0) if n < 2 else (packed_ref, MAIN * (TILES - 1))
            for t in range(TILES - 1):
                if n == 2:
                    target[t * MAIN : (t + 1) * MAIN, :] = main_ref[:, t * HC : (t + 1) * HC]
                target[base + t * KEPT : base + (t + 1) * KEPT, :] = strip[:, t * HC : (t + 1) * HC]
            target[base + STRIP : base + STRIP + HR, :] = upper
            target[base + STRIP + HR : base + STRIP + SIDE, :] = lower
    sensor_ref[...] = packed_ref[pl.ds(pl.multiple_of(at_ref[TARGET], PAD), CHUNK), :]


def cut_strips(at, *blocks):
    return pl.pallas_call(
        strips_kernel,
        out_shape=(f32(2, STRIP + SIDE, HC),) * 4 + (f32(CHUNK, HC),),
        in_specs=[SMEM] + [VMEM] * 5,
        out_specs=(VMEM,) * 5,
        scratch_shapes=[pltpu.VMEM((ROWS + HR + 2 * HC - WINDOW, HC), jnp.float32), pltpu.VMEM((PACKED, HC), jnp.float32), TURNED],
        name="strips",
        compiler_params=grant(20),
    )(at, *near(*blocks))


def sum_kernel(*refs):
    refs[-1][...] = (refs[0][...] + refs[1][...]) + (refs[2][...] + refs[3][...])


def summed(blocks):
    return pl.pallas_call(
        sum_kernel,
        out_shape=f32(*blocks[0].shape),
        in_specs=[VMEM] * 4,
        out_specs=VMEM,
        name="summed",
        compiler_params=grant(8),
    )(*near(*blocks))


def first_ratio_kernel(mine_ref, other_ref, sensor_ref, ratio_ref, count_ref):
    count = mine_ref[0] + other_ref[0]
    count_ref[...] = count
    ratio_ref[...] = (sensor_ref[...] - (mine_ref[1] + other_ref[1])) / count


def ratio_kernel(mine_ref, other_ref, sensor_ref, count_ref, ratio_ref):
    ratio_ref[...] = (sensor_ref[...] - (mine_ref[...] + other_ref[...])) / count_ref[...]


def ratio_of(first, *blocks):
    chunk = f32(CHUNK, HC)
    return pl.pallas_call(
        first_ratio_kernel if first else ratio_kernel,
        out_shape=(chunk, chunk) if first else chunk,
        in_specs=[VMEM] * len(blocks),
        out_specs=(VMEM, VMEM) if first else VMEM,
        name="first_ratio" if first else "ratio",
        compiler_params=grant(8),
    )(*near(*blocks))


def packed_parts():
    base = MAIN * (TILES - 1)
    for t in range(TILES - 1):
        yield t, slice(t * MAIN, (t + 1) * MAIN), 0, (slice(0, MAIN), slice(t * HC, (t + 1) * HC))
    for t in range(TILES - 1):
        yield t, slice(base + t * KEPT, base + (t + 1) * KEPT), 1, (slice(t * KEPT, (t + 1) * KEPT), slice(None))
    yield None, slice(base + STRIP, PACKED), 1, (slice(STRIP, STRIP + SIDE), slice(None))


def tiled_place(t, source, row, col):
    if source == 0:
        return col + t, pl.ds(pl.multiple_of(row * HR, HR), MAIN)
    return col + t, pl.ds(pl.multiple_of((1 - row) * MAIN, HR), HR)


def write_pieces(at_ref, whole_ref, outs):
    for k, out in enumerate(outs):
        piece = (pl.ds(pl.multiple_of(at_ref[TARGET + k], PAD), CHUNK), slice(None))
        for n in range(2) if len(out.shape) == 3 else (None,):
            lead = () if n is None else (n,)
            out[lead + (slice(None), slice(None))] = whole_ref[lead + piece]


def tally_kernel(at_ref, *refs):
    pairs, outs, sums_ref = refs[:8], refs[8:12], refs[12]
    for _, packed, source, cut in packed_parts():
        count = 0.0
        measured = 0.0
        for k in range(4):
            masks = pairs[2 * k + source][(0,) + cut]
            count += masks * masks
            measured += masks * pairs[2 * k + source][(1,) + cut]
        sums_ref[0, packed, :] = count
        sums_ref[1, packed, :] = measured
    write_pieces(at_ref, sums_ref, outs)


def tally(at, pairs):
    return pl.pallas_call(
        tally_kernel,
        out_shape=(f32(2, CHUNK, HC),) * 4,
        in_specs=[SMEM] + [VMEM] * 8,
        out_specs=(VMEM,) * 4,
        scratch_shapes=[pltpu.VMEM((2, PACKED, HC), jnp.float32)],
        name="tally",
        compiler_params=grant(20),
    )(at, *near(*pairs))


def tv_steps(f_ref, pr_ref, pc_ref, w_ref, frame, at, rows):
    tiles, _, lanes = f_ref.shape[1:]
    lane = lax.broadcasted_iota(jnp.int32, (rows, lanes), 1)

    def dual():
        before = 0.0
        for t in range(tiles):
            pc = pc_ref[t, :rows, :]
            turned = pltpu.roll(pc, 1, 1)
            left = jnp.where(lane == 0, before, turned)
            before = turned
            pr = pr_ref[t, PAD : PAD + rows, :]
            up = pr_ref[t, PAD - 1 : PAD - 1 + rows, :]
            w_ref[t, :rows, :] = step_size * ((pr - up) + (pc - left)) - f_ref[frame, t, pl.ds(at, rows), :]
        w_ref[:, rows : rows + 1, :] = w_ref[:, rows - 1 : rows, :]

    def update(start):
        for r in range(0, rows, BLOCK):
            n = min(BLOCK, rows - r)
            turned = pltpu.roll(w_ref[0, r : r + n, :], lanes - 1, 1)
            for t in range(tiles):
                w = w_ref[t, r : r + n, :]
                following = pltpu.roll(w_ref[t + 1, r : r + n, :], lanes - 1, 1) if t + 1 < tiles else w
                right = jnp.where(lane[:n] == lanes - 1, following, turned)
                turned = following
                gr = w_ref[t, r + 1 : r + n + 1, :] - w
                gc = right - w
                s = gr * gr + gc * gc
                inv = 1.0 / (1.0 + s * lax.rsqrt(jnp.maximum(s, TINY)))
                if not start:
                    gr = pr_ref[t, PAD + r : PAD + r + n, :] + gr
                    gc = pc_ref[t, r : r + n, :] + gc
                pr_ref[t, PAD + r : PAD + r + n, :] = gr * inv
                pc_ref[t, r : r + n, :] = gc * inv

    for t in range(tiles):
        w_ref[t, :rows, :] = -f_ref[frame, t, pl.ds(at, rows), :]
    w_ref[:, rows : rows + 1, :] = w_ref[:, rows - 1 : rows, :]
    update(True)

    def iteration(_, carry):
        dual()
        update(False)
        return carry

    lax.fori_loop(1, TV_ITERS, iteration, 0)
    dual()


def load_ratio(at_ref, ratios, ratio_ref):
    for k, ratio in enumerate(ratios):
        ratio_ref[pl.ds(pl.multiple_of(at_ref[SOURCE + k], PAD), CHUNK), :] = ratio[...]


def first_kernel(at_ref, *refs):
    pairs, ratios, videos, products = refs[:8], refs[8:12], refs[12:16], refs[16:20]
    ratio_ref, f_ref, pr_ref, pc_ref, w_ref, turned_ref, product_ref, rows_ref = refs[20:]
    row = at_ref[ROW]
    col = at_ref[COL]
    halo = (1 - col) * (TILES - 1)
    load_ratio(at_ref, ratios, ratio_ref)
    turned_ref[...] = jnp.zeros((HC, 2 * HC), jnp.float32)
    scale = step_size / tv_weight
    pr_ref[:, :PAD, :] = jnp.zeros((TILES, PAD, HC), jnp.float32)
    for k in range(4):
        for t, packed, source, cut in packed_parts():
            pair = pairs[2 * k + source]
            noisy = scale * (pair[(1,) + cut] + pair[(0,) + cut] * ratio_ref[packed, :])
            if t is None:
                f_ref[k, halo, :HC, :], f_ref[k, halo, HC:, :] = halo_tile(noisy, turned_ref, col)
            else:
                tile, rows = tiled_place(t, source, row, col)
                f_ref[k, tile, rows, :] = strip_rows(noisy, row) if source else noisy

    def one(k, carry):
        tv_steps(f_ref, pr_ref, pc_ref, w_ref, k, 0, WINDOW)
        for t in range(TILES):
            f_ref[k, t] = (-tv_weight / step_size) * w_ref[t, :WINDOW, :]
        return carry

    lax.fori_loop(0, 4, one, 0)
    rows_ref[WINDOW:, :] = jnp.zeros((2 * HC - WINDOW, HC), jnp.float32)
    for t, packed, source, cut in packed_parts():
        product = 0.0
        for k in range(4):
            if t is None:
                rows_ref[:WINDOW, :] = f_ref[k, halo]
                video = jnp.concatenate(turn_side(rows_ref[...], turned_ref, col), 0)
            else:
                tile, rows = tiled_place(t, source, row, col)
                video = f_ref[k, tile, rows, :]
                video = kept_rows(video, row) if source else video
            product += video * pairs[2 * k + source][(0,) + cut]
        product_ref[packed, :] = product
    for k in range(4):
        videos[k][...] = f_ref[k]
    write_pieces(at_ref, product_ref, products)


def tv_scratch(frames):
    return [
        pltpu.VMEM((PACKED, HC), jnp.float32),
        pltpu.VMEM((frames, TILES, WINDOW, HC), jnp.float32),
        pltpu.VMEM((TILES, WINDOW + 8, HC), jnp.float32),
        pltpu.VMEM((TILES, WINDOW + 16, HC), jnp.float32),
        pltpu.VMEM((TILES, WINDOW + 24, HC), jnp.float32),
        TURNED,
    ]


def first_denoise(at, pairs, ratios):
    out = pl.pallas_call(
        first_kernel,
        out_shape=(f32(TILES, WINDOW, HC),) * 4 + (f32(CHUNK, HC),) * 4,
        in_specs=[SMEM] + [VMEM] * 12,
        out_specs=(VMEM,) * 8,
        scratch_shapes=tv_scratch(4) + [pltpu.VMEM((PACKED, HC), jnp.float32), pltpu.VMEM((2 * HC, HC), jnp.float32)],
        name="tv_first",
        compiler_params=grant(36),
    )(at, *near(*pairs, *ratios))
    return out[:4], out[4:]


def last_kernel(at_ref, main_ref, strip_ref, video_ref, *refs):
    ratios, out_ref = refs[:4], refs[4]
    ratio_ref, f_ref, pr_ref, pc_ref, w_ref, turned_ref = refs[5:]
    row = at_ref[ROW]
    col = at_ref[COL]
    halo = (1 - col) * (TILES - 1)
    load_ratio(at_ref, ratios, ratio_ref)
    turned_ref[...] = jnp.zeros((HC, 2 * HC), jnp.float32)
    scale = step_size / tv_weight
    pr_ref[:, :PAD, :] = jnp.zeros((TILES, PAD, HC), jnp.float32)
    pair = (main_ref, strip_ref)
    for t, packed, source, cut in packed_parts():
        change = pair[source][(0,) + cut] * ratio_ref[packed, :]
        if t is None:
            upper, lower = halo_tile(change, turned_ref, col)
            f_ref[0, halo, :HC, :] = scale * (video_ref[halo, :HC, :] + upper)
            f_ref[0, halo, HC:, :] = scale * (video_ref[halo, HC:, :] + lower)
        else:
            tile, rows = tiled_place(t, source, row, col)
            change = strip_rows(change, row) if source else change
            f_ref[0, tile, rows, :] = scale * (video_ref[tile, rows, :] + change)
    half = pl.multiple_of(at_ref[HALF], PAD)
    tv_steps(f_ref, pr_ref, pc_ref, w_ref, 0, half, MAIN)
    for t in range(TILES - 1):
        out_ref[:, t * HC : (t + 1) * HC] = (-tv_weight / step_size) * w_ref[col + t, pl.ds(half, QUARTER), :]


def last_denoise(at, pair, video, ratios):
    return pl.pallas_call(
        last_kernel,
        out_shape=f32(QUARTER, COLS),
        in_specs=[SMEM] + [VMEM] * 7,
        out_specs=VMEM,
        scratch_shapes=tv_scratch(1),
        name="tv_last",
        compiler_params=grant(16),
    )(at, *near(*pair, video, *ratios))


def join_kernel(at_ref, *refs):
    blocks, out_ref, sems = refs[:4], refs[4], refs[5]
    copies = []
    for k, block in enumerate(blocks):
        place = out_ref.at[pl.ds(pl.multiple_of(at_ref[PLACE + k], QUARTER), QUARTER), :]
        copies.append(pltpu.make_async_copy(block, place, sems.at[k]))
        copies[-1].start()
    for one in copies:
        one.wait()


def join(at, blocks):
    return pl.pallas_call(
        join_kernel,
        out_shape=f32(ROWS, COLS),
        in_specs=[SMEM] + [VMEM] * 4,
        out_specs=HBM,
        scratch_shapes=[pltpu.SemaphoreType.DMA((4,))],
        name="join",
        compiler_params=grant(8),
    )(at, *near(*blocks))


def table(*values):
    return jnp.stack([jnp.asarray(value, jnp.int32) for value in values])


def per_device(measurement, masks, estimate):
    masks = masks[0]
    video = estimate[0]
    row = lax.axis_index("row")
    col = lax.axis_index("col")
    frame = lax.axis_index("frame")
    z, x = frame // 8, (frame // 2) % 4
    mine = jnp.where(col == 0, z, x)
    other = jnp.where(col == 0, x, z)

    starts = [window_start((mine + turn) % 4, row) for turn in (0,) + TURNS]
    strip_at = [jnp.where(row == 0, jnp.minimum(start + MAIN, ROWS - HR), jnp.maximum(start - HR, 0)) for start in starts]
    outside = [start == (ROWS - MAIN) * (1 - row) for start in starts]
    sources = [(other - turn) % 4 * CHUNK for turn in (0,) + TURNS]
    targets = [(other + turn) % 4 * CHUNK for turn in (0,) + TURNS]
    half = (mine * QUARTER - HR * (1 - row) - starts[0] + HR) // 2
    places = [(mine + turn) % 4 * QUARTER for turn in (0,) + TURNS]
    at = table(row, col, *starts, *strip_at, *outside, *sources, *targets, half, *places)

    *mains, strips, sensor, edge, end, corner = cut(at, masks, video, measurement)
    mains = [mains[0]] + [hop(mains[1 + n], 0, turn) for n, turn in enumerate(TURNS)]
    swap = [(0, 1), (1, 0)]
    beside = lax.ppermute(edge, "col", swap)
    below = lax.ppermute(end, "row", swap)
    corner = lax.ppermute(corner, ("row", "col"), [(0, 3), (3, 0), (1, 2), (2, 1)])
    *strips, sensor = cut_strips(at, strips, sensor, beside, below, corner)
    strips = [strips[0]] + [hop(strips[1 + n], 0, turn) for n, turn in enumerate(TURNS)]
    pairs = [block for both in zip(mains, strips) for block in both]

    def total(pieces):
        got = summed([pieces[0]] + [hop(piece, 1, turn) for piece, turn in zip(pieces[1:], TURNS)])
        return got, hop(got, 2, 1)

    def spread(chunk):
        return [chunk] + [hop(chunk, 1, turn) for turn in TURNS]

    sums = total(tally(at, pairs))
    ratio, count = ratio_of(True, *sums, sensor)
    videos, products = first_denoise(at, pairs, spread(ratio))
    ratios = spread(ratio_of(False, *total(products), sensor, count))
    blocks = []
    for n, turn in enumerate(TURNS):
        blocks.append(hop(last_denoise(at, pairs[2 + 2 * n : 4 + 2 * n], videos[1 + n], ratios), 0, 4 - turn))
    own = last_denoise(at, pairs[:2], videos[0], ratios)
    return join(at, [own] + blocks)[None]


def solution(mesh):
    return jax.shard_map(
        per_device,
        mesh=mesh,
        in_specs=(P("row", "col"), P("frame", "row", "col"), P("frame", "row", "col")),
        out_specs=P("frame", "row", "col"),
        check_vma=False,
    )
```
